128 devices in a mesh: section: 2 (over core), dp: 32 (over z, y, x_lo), mp: 2 (over x_hi).
Axes of the slice: x: 4 (x_hi: 2, x_lo: 2; x = x_hi * 2 + x_lo), y: 4, z: 4, core: 2. Of those that a mesh axis runs over, the one named last changes fastest.
Arguments:
- states: bfloat16 [2, 64, 128, 2816], P('section', 'dp'), may hold values from -8 to 8
- injection: bfloat16 [64, 128, 2816], P('dp', None, 'mp'), may hold values from -2.390625 to 2.390625
- cotangent: bfloat16 [64, 128, 2816], P('dp', None, 'mp'), may hold values from -6 to 6
- gain: float32 [2816], P('mp'), may hold values from 0.5 to 1.5
- weight: bfloat16 [2816, 2816], P(None, 'mp'), may hold values from -0.109375 to 0.109375
- exits: int32 [64], P('dp'), may hold values from 1 to 2, as said below
- order: int32 [32, 2], P('dp'), may hold values from 0 to 1, each once within a row
Outputs:
- d_injection: float32 [64, 128, 2816], P('dp', None, 'mp')
- d_weight: float32 [2816, 2816], P(('section', 'dp'), 'mp')
- d_gain: float32 [2816], P('mp')
The draws below stay inside these ranges and needn't reach their ends.
Inputs may be any that keep to these rules, and one draw needn't show every extreme that they name: `exits`: some micro-batch runs all 2 iterations and some only one. `order`: each row is a permutation of 0 .. 1.
All inputs are finite; a program needn't handle non-finite values.
Results may differ from the reference program's by a relative error of at most 0.0033.
Values may be sent and summed in bfloat16 or wider, within the bound.
A program may use at most 128 MiB of HBM per device.

```python
import jax
import jax.numpy as jnp
from jax import lax

D = 2816
MBD = 2
ROWS = 128
LOOPS = 2
MICRO = 64
N_DP = 32


def draw_exits(key, part):
    key_values, key_order = jax.random.split(key)
    values = jax.random.randint(key_values, (MICRO,), 1, LOOPS + 1)
    shuffled = jax.random.permutation(key_order, MICRO)
    values = values.at[shuffled[0]].set(LOOPS)
    values = values.at[shuffled[1]].set(1)
    return values.astype(jnp.int32)


def with_spikes(drawn, rng, source, target, parts, factor):
    def block_of(position):
        return (jnp.arange(drawn.shape[position]) // (drawn.shape[position] // parts)).reshape((-1,) + (1,) * (drawn.ndim - 1 - position))

    near = jax.random.permutation(rng, parts)[block_of(target)]
    second = (block_of(target) + parts // 2) % parts
    return jnp.where((block_of(source) == near) | (block_of(source) == second), factor * drawn, drawn)


def level_of(key, dims, shards, least, largest):
    def one(dim, shards_of):
        draws = jax.random.uniform(jax.random.fold_in(jax.random.fold_in(key, 6), dim), (shards_of,), jnp.float32, least / len(shards), largest / len(shards))
        return jnp.repeat(jnp.exp(draws), dims[dim] // shards_of).reshape((-1,) + (1,) * (len(dims) - dim - 1))

    level = one(*shards[0])
    for cut in shards[1:]:
        level = level * one(*cut)
    return level


def scatter_about(own_key, dims, spread, reach, cuts=(), kind=jnp.bfloat16):
    factor_of = level_of(own_key, dims, cuts, -0.22, 0.18) if cuts else 1.0
    entries = jax.random.normal(own_key, dims, jnp.float32) * spread * factor_of
    return jnp.minimum(jnp.maximum(entries, -reach), reach).astype(kind)


def heavy_noise(key, dims, scale, limit, cuts, heavy, kind=jnp.bfloat16):
    values = scale * jax.random.normal(key, dims, jnp.float32)
    if cuts:
        values = values * level_of(key, dims, cuts, -0.22, 0.18)
    return jnp.clip(with_spikes(values, jax.random.fold_in(key, 3), *heavy), -limit, limit).astype(kind)


def setup_inputs(seed: int = 0) -> dict:
    splits = jax.random.split(jax.random.key(seed), 8)
    states = heavy_noise(splits[0], (LOOPS, MICRO, ROWS, D), 1.0, 8.0, ((0, 2), (1, 32)), (0, 3, 2, 2.0))
    injection = scatter_about(splits[1], (MICRO, ROWS, D), 0.3, 2.390625, ((0, 32), (2, 2)))
    cotangent = scatter_about(splits[2], (MICRO, ROWS, D), 1.0, 6.0, ((0, 32), (2, 2)))
    gain = jnp.clip(1.0 + 0.1 * jax.random.normal(splits[3], (D,), jnp.float32), 0.5, 1.5)
    weight = scatter_about(splits[4], (D, D), D ** -0.5, 0.109375, ((1, 2),))
    exits = draw_exits(jax.random.fold_in(splits[7], 71), 0)
    order = jax.vmap(lambda own: jax.random.permutation(own, MBD))(jax.random.split(splits[6], N_DP)).reshape((N_DP, MBD)).astype(jnp.int32)
    return dict(states=states, injection=injection, cotangent=cotangent, gain=gain, weight=weight, exits=exits, order=order)


epsilon = 1e-06

def reference(states, injection, cotangent, gain, weight, exits, order):
    slot_micro = (jnp.arange(N_DP, dtype=jnp.int32)[:, None] * MBD + order).reshape(-1).astype(jnp.int32)

    def per_slot(slot, outer):
        d_weight, d_gain, d_injection = outer
        micro_id = slot_micro[slot]
        exit_count = exits[micro_id]
        inj_rows = injection[micro_id].astype(jnp.float32)
        start_grad = cotangent[micro_id].astype(jnp.float32)

        def per_iter(step_num, inner_state):
            carried, weight_acc, gain_acc, inj_acc = inner_state
            level = (exit_count - 1 - step_num).astype(jnp.int32)
            stashed = states[level, slot]
            pre_norm = jnp.dot(stashed, weight, preferred_element_type=jnp.float32) + inj_rows
            scaled = carried * gain
            squares = lax.optimization_barrier(jnp.sum(pre_norm * pre_norm, axis=1))
            inner_sum = lax.optimization_barrier(jnp.sum(scaled * pre_norm, axis=1))
            radius = jnp.sqrt(squares / D + epsilon)
            normed = pre_norm / radius[:, None]
            delta_pre = (scaled - normed * (inner_sum / (radius * D))[:, None]) / radius[:, None]
            delta_bf = delta_pre.astype(jnp.bfloat16)
            new_grad = jnp.dot(delta_bf, weight.T, preferred_element_type=jnp.float32).astype(jnp.bfloat16)
            new_grad = lax.optimization_barrier(new_grad).astype(jnp.float32)
            weight_acc = weight_acc + jnp.dot(stashed.T, delta_bf, preferred_element_type=jnp.float32)
            gain_acc = gain_acc + lax.optimization_barrier(jnp.sum(carried * normed, axis=0))
            return (new_grad, weight_acc, gain_acc, inj_acc + delta_pre)
        zero_inj = jnp.zeros((ROWS, D), jnp.float32)
        result = lax.fori_loop(0, exit_count, per_iter, (start_grad, d_weight, d_gain, zero_inj))
        d_injection = d_injection.at[micro_id].set(result[3])
        return (result[1], result[2], d_injection)
    init_state = (jnp.zeros((D, D), jnp.float32), jnp.zeros((D,), jnp.float32), jnp.zeros((MICRO, ROWS, D), jnp.float32))
    d_weight, d_gain, d_injection = lax.fori_loop(0, MICRO, per_slot, init_state)
    return (d_injection, d_weight, d_gain)
```

```python
import functools

import jax
import jax.numpy as jnp
from jax import lax
from jax.experimental import pallas as pl
from jax.experimental.pallas import tpu as pltpu
from jax.sharding import PartitionSpec as P

MESH = pl.DeviceIdType.MESH
F32 = jnp.float32
BF16 = jnp.bfloat16
epsilon = 1e-06

D = 2816
H = 1408
R = 128
N = 256
CA = 768
CB = H - CA
CHUNKS = ((0, 256), (256, 256), (512, 256), (768, 256), (1024, 256), (1280, 128))
RB = 32


def kernel(names, *refs):
    r = dict(zip(names, refs))
    order, exits, gain = r["order"], r["exits"], r["gain"]
    s = lax.axis_index("section")
    d = lax.axis_index("dp")
    h = lax.axis_index("mp")
    z, y, xl = d // 8, (d // 2) % 4, d % 2

    def dev(s_, z_, y_, x_, h_):
        return (s_, z_ * 8 + y_ * 2 + x_, h_)

    core = dev(1 - s, z, y, xl, h)
    part = dev(s, z, y, xl, 1 - h)
    cross = dev(1 - s, z, y, xl, 1 - h)
    zdev = [dev(s, (z + t) % 4, y, xl, h) for t in (1, 2, 3)]
    ydev = [dev(s, z, (y + t) % 4, xl, h) for t in (1, 2, 3)]
    xdev = dev(s, z, y, 1 - xl, h)

    def rcopy(src, dst, ss, rs, to):
        return pltpu.make_async_remote_copy(src, dst, ss, rs, device_id=to, device_id_type=MESH)

    swapped = order[0, 0] != 0
    first, second = exits[0], exits[1]
    exit_of = (jnp.where(swapped, second, first), jnp.where(swapped, first, second))

    def by_slot(name, j, rows, cols):
        kept = r[name][j, rows, cols].astype(F32)
        other = r[name][1 - j, rows, cols].astype(F32)
        return jnp.where(swapped, other, kept)

    loc = r["loc"]
    cp_st = pltpu.make_async_copy(r["states"].at[0], r["st"], loc.at[0])
    cp_inj = pltpu.make_async_copy(r["inj"], r["injv"], loc.at[1])
    cp_cot = pltpu.make_async_copy(r["cot"], r["cotv"], loc.at[2])
    cp_w = [
        pltpu.make_async_copy(r["w"].at[:, pl.ds(c0, cw)], r["wv"].at[:, pl.ds(c0, cw)], loc.at[3 + i])
        for i, (c0, cw) in enumerate(CHUNKS)
    ]
    cp_st.start()
    cp_w[0].start()
    cp_inj.start()
    cp_cot.start()
    for c in cp_w[1:]:
        c.start()

    barrier = pltpu.get_barrier_semaphore()
    everyone = [core, part, cross, xdev] + zdev + ydev
    for p in everyone:
        pl.semaphore_signal(barrier, 1, device_id=p, device_id_type=MESH)
    pl.semaphore_wait(barrier, len(everyone))

    other_half = pl.multiple_of((1 - s) * H, 128)
    cp_sx = rcopy(r["states"].at[0, :, :, pl.ds(other_half, H)], r["stx"], r["sxs"], r["sxr"], core)
    cp_sx.start()

    cp_st.wait()
    cp_inj.wait()
    cp_cot.wait()
    av = r["av"]
    for i, (c0, cw) in enumerate(CHUNKS):
        cp_w[i].wait()
        prod = jnp.dot(r["st"][...].reshape(N, D), r["wv"][:, c0 : c0 + cw], preferred_element_type=F32)
        for j in range(2):
            inj = by_slot("injv", j, slice(None), slice(c0, c0 + cw))
            av[pl.ds(j * R, R), c0 : c0 + cw] = prod[j * R : (j + 1) * R] + inj

    def lanes_sum(v):
        t = v[:, 0:128]
        for q in range(1, H // 128):
            t = t + v[:, q * 128 : (q + 1) * 128]
        return t

    def widen(v):
        return jnp.concatenate([v] * (H // 128), axis=1)

    def rowform(ref):
        return jnp.sum(jnp.transpose(ref[...]), axis=0, keepdims=True)

    def colform(row):
        return jnp.transpose(jnp.broadcast_to(row, (128, N)))

    gain_row = gain[...]

    def row_loop(step, init):
        carry = init
        for j in range(2):
            carry = lax.fori_loop(
                0,
                R // RB,
                lambda q, c, j=j: step(
                    pl.ds(pl.multiple_of(j * R + q * RB, RB), RB), j, pl.ds(pl.multiple_of(q * RB, RB), RB), c
                ),
                carry,
            )
        return carry

    def stat_step(rows, j, inner_rows, carry):
        a = av[rows, :]
        r["colq"][rows, :] = lanes_sum(a * a)
        u = by_slot("cotv", j, inner_rows, slice(None)) * gain_row
        r["coli"][rows, :] = lanes_sum(u * a)
        return carry

    row_loop(stat_step, 0)
    r["srow"][0:1, :] = rowform(r["colq"])
    r["srow"][1:2, :] = rowform(r["coli"])
    cp_stat = rcopy(r["srow"], r["rrow"], r["sts"].at[0], r["str"].at[0], part)
    cp_stat.start()

    cp_db = rcopy(r["db"], r["dbx"], r["dbs"], r["dbr"], core)
    cp_da = rcopy(r["da"], r["dax"], r["das"], r["dar"], core)
    cp_po = rcopy(r["po"], r["pox"], r["pos"], r["por"], core)
    cp_pc = rcopy(r["pc"], r["pcx"], r["pcs"], r["pcr"], cross)
    cp_in = rcopy(r["irow"], r["irx"], r["sts"].at[1], r["str"].at[1], part)

    def transpose_half(get, out):
        for q in range(H // 128):
            r["stt"][pl.ds(q * 128, 128), :] = jnp.transpose(get(q).astype(F32))
        for b in range(32):
            blk = r["stt"][b * 44 : b * 44 + 44, :].astype(BF16)
            out[b // 8, (b // 2) % 4, (b % 2) * 48 : (b % 2) * 48 + 44, :] = blk

    def build_own(k):
        own_half = pl.multiple_of(s * H, 128)
        transpose_half(
            lambda q: r["st"][:, :, pl.ds(pl.multiple_of(own_half + q * 128, 128), 128)].reshape(N, 128),
            r["stp"].at[k],
        )

    def build_other(k):
        cp_sx.wait_recv()
        transpose_half(lambda q: r["stx"][:, :, q * 128 : (q + 1) * 128].reshape(N, 128), r["stp"].at[k])

    def early_product(dbref):
        def step(zi, carry):
            lhs = r["stp"][1, zi].reshape(384, N)
            for c0, cw in CHUNKS:
                r["p1"][zi, :, :, c0 : c0 + cw] = jnp.dot(
                    lhs, dbref[:, c0 : c0 + cw], preferred_element_type=F32
                ).reshape(4, 96, cw)
            return carry

        lax.fori_loop(0, 4, step, 0)

    def norm_columns(sq_row, in_row):
        inv = 1.0 / jnp.sqrt(sq_row * (1.0 / D) + epsilon)
        r["colq"][...] = colform(inv)
        r["coli"][...] = colform(in_row * inv * (1.0 / D))

    def finish_da(get_c, mask_all):
        def step(rows, j, inner_rows, acc):
            inv = widen(r["colq"][rows, :])
            n = av[rows, :] * inv
            c = get_c(rows, j, inner_rows)
            da = (c * gain_row - n * widen(r["coli"][rows, :])) * inv
            g = c * n
            if mask_all:
                live = exit_of[j] > 1
                da = jnp.where(live, da, 0.0)
                g = jnp.where(live, g, 0.0)
            r["da"][rows, :] = da
            r["db"][rows, :] = da.astype(BF16)
            return acc + jnp.sum(g.reshape(RB // 8, 8, H), axis=0)

        acc = row_loop(step, jnp.zeros((8, H), F32))
        r["gc"][s] = jnp.sum(acc, axis=0, keepdims=True)

    @pl.when(s == 1)
    def _():
        cp_stat.wait_recv()
        tot = r["srow"][...] + r["rrow"][...]
        norm_columns(tot[0:1], tot[1:2])
        finish_da(lambda rows, j, ir: by_slot("cotv", j, ir, slice(None)), True)
        cp_db.start()
        away = pl.multiple_of((1 - h) * H, 128)
        for c0, cw in CHUNKS:
            r["pc"][:, c0 : c0 + cw] = lax.dot_general(
                r["db"][...], r["wv"][pl.ds(away + c0, cw), :], (((1,), (1,)), ((), ())), preferred_element_type=F32
            ).astype(BF16)
        cp_pc.start()
        home = pl.multiple_of(h * H, 128)
        for c0, cw in CHUNKS:
            r["po"][:, c0 : c0 + cw] = lax.dot_general(
                r["db"][...], r["wv"][pl.ds(home + c0, cw), :], (((1,), (1,)), ((), ())), preferred_element_type=F32
            )
        cp_po.start()
        cp_da.start()
        build_own(1)
        build_other(0)
        early_product(r["db"])
        cp_po.wait_send()
        cp_pc.wait_send()
        cp_db.wait()

    @pl.when(s == 0)
    def _():
        build_own(0)
        build_other(1)
        cp_db.wait_recv()
        early_product(r["dbx"])
        cp_stat.wait_recv()
        cp_po.wait_recv()
        cp_pc.wait_recv()

        def inner_step(rows, j, ir, carry):
            start = jnp.where(exit_of[j] == 1, by_slot("cotv", j, ir, slice(None)), 0.0)
            c = r["pox"][rows, :] + r["pcx"][rows, :].astype(F32) + start
            r["pox"][rows, :] = c
            r["coli"][rows, :] = lanes_sum(c * gain_row * av[rows, :])
            return carry

        row_loop(inner_step, 0)
        r["irow"][0:1, :] = rowform(r["coli"])
        cp_in.start()
        cp_in.wait()
        sq = r["srow"][0:1] + r["rrow"][0:1]
        norm_columns(sq, r["irow"][0:1] + r["irx"][0:1])
        finish_da(lambda rows, j, ir: r["pox"][rows, :], False)
        cp_db.start()
        cp_da.start()
        cp_db.wait_send()

    cp_stat.wait_send()

    dbl = r["dbl"]

    @pl.when(s == 0)
    def _():
        dbl[...] = r["db"][...]

    @pl.when(s == 1)
    def _():
        dbl[...] = r["dbx"][...]

    def pieces(v, cw):
        return v.reshape(4, 2, 48, cw)[:, :, 0:44, :]

    a1 = []
    b1 = []
    for t in (1, 2, 3, 4):
        zd = (z + t) % 4
        yd = (y + t) % 4
        va = jnp.dot(r["stp"][0, zd].reshape(384, N), dbl[:, 0:CA], preferred_element_type=F32)
        va = va + r["p1"][zd, :, :, 0:CA].reshape(384, CA)
        if t < 4:
            r["pa"][t - 1] = pieces(va, CA).astype(BF16)
            a1.append(rcopy(r["pa"].at[t - 1], r["ra"].at[t - 1], r["a1s"].at[t - 1], r["a1r"].at[t - 1], zdev[t - 1]))
            a1[-1].start()
        else:
            r["oa"][...] = pieces(va, CA)
        vb = jnp.dot(r["stp"][0, :, yd].reshape(384, N), dbl[:, CA:H], preferred_element_type=F32)
        vb = vb + r["p1"][:, yd, :, CA:H].reshape(384, CB)
        if t < 4:
            r["pb"][t - 1] = pieces(vb, CB).astype(BF16)
            b1.append(rcopy(r["pb"].at[t - 1], r["rb"].at[t - 1], r["b1s"].at[t - 1], r["b1r"].at[t - 1], ydev[t - 1]))
            b1[-1].start()
        else:
            r["ob"][...] = pieces(vb, CB)

    cp_gc = rcopy(r["gc"].at[s], r["gc"].at[s], r["gs"].at[0], r["gr"].at[0], core)
    cp_gc.start()

    cp_da.wait_recv()
    def inj_step(q, carry):
        tot = []
        for j in range(2):
            rows = pl.ds(pl.multiple_of(j * R + q * RB, RB), RB)
            tot.append(r["da"][rows, :] + r["dax"][rows, :])
        rows = pl.ds(pl.multiple_of(q * RB, RB), RB)
        r["dinj"][0, rows, :] = jnp.where(swapped, tot[1], tot[0])
        r["dinj"][1, rows, :] = jnp.where(swapped, tot[0], tot[1])
        return carry

    lax.fori_loop(0, R // RB, inj_step, 0)
    cp_da.wait_send()

    rcopy(r["gc"].at[1 - s], r["gc"].at[1 - s], r["gs"].at[0], r["gr"].at[0], core).wait_recv()
    cp_gc.wait_send()
    r["gz"][z] = r["gc"][0] + r["gc"][1]
    gz = [rcopy(r["gz"].at[z], r["gz"].at[z], r["gs"].at[t], r["gr"].at[t], zdev[t - 1]) for t in (1, 2, 3)]
    for c in gz:
        c.start()

    for c in a1 + b1:
        c.wait()
    a2 = []
    b2 = []
    for t in (1, 2, 3, 4):
        yd = (y + t) % 4
        zd = (z + t) % 4
        va = r["oa"][yd]
        vb = r["ob"][zd]
        for k in range(3):
            va = va + r["ra"][k, yd].astype(F32)
            vb = vb + r["rb"][k, zd].astype(F32)
        if t < 4:
            r["pa2"][t - 1] = va.astype(BF16)
            a2.append(rcopy(r["pa2"].at[t - 1], r["ra2"].at[t - 1], r["a2s"].at[t - 1], r["a2r"].at[t - 1], ydev[t - 1]))
            a2[-1].start()
            r["pb2"][t - 1] = vb.astype(BF16)
            b2.append(rcopy(r["pb2"].at[t - 1], r["rb2"].at[t - 1], r["b2s"].at[t - 1], r["b2r"].at[t - 1], zdev[t - 1]))
            b2[-1].start()
        else:
            r["oa2"][...] = va
            r["ob2"][...] = vb

    for t in (1, 2, 3):
        zs = (z + 4 - t) % 4
        rcopy(r["gz"].at[zs], r["gz"].at[zs], r["gs"].at[t], r["gr"].at[t], zdev[t - 1]).wait_recv()
    for c in gz:
        c.wait_send()
    r["gy"][y] = r["gz"][0] + r["gz"][1] + r["gz"][2] + r["gz"][3]
    gy = [rcopy(r["gy"].at[y], r["gy"].at[y], r["gs"].at[3 + t], r["gr"].at[3 + t], ydev[t - 1]) for t in (1, 2, 3)]
    for c in gy:
        c.start()

    for c in a2 + b2:
        c.wait()
    for t in (1, 2, 3):
        ys = (y + 4 - t) % 4
        rcopy(r["gy"].at[ys], r["gy"].at[ys], r["gs"].at[3 + t], r["gr"].at[3 + t], ydev[t - 1]).wait_recv()
    for c in gy:
        c.wait_send()
    r["gx"][xl] = r["gy"][0] + r["gy"][1] + r["gy"][2] + r["gy"][3]
    cp_gx = rcopy(r["gx"].at[xl], r["gx"].at[xl], r["gs"].at[7], r["gr"].at[7], xdev)
    cp_gx.start()

    def third(q):
        va = r["oa2"][q]
        vb = r["ob2"][q]
        for k in range(3):
            va = va + r["ra2"][k, q].astype(F32)
            vb = vb + r["rb2"][k, q].astype(F32)
        return va, vb

    va, vb = third(1 - xl)
    r["p3"][:, 0:CA] = va.astype(BF16)
    r["p3"][:, CA:H] = vb.astype(BF16)
    cp_3 = rcopy(r["p3"], r["r3"], r["x3s"], r["x3r"], xdev)
    cp_3.start()
    va, vb = third(xl)
    cp_3.wait()
    r["dw"][:, 0:CA] = va + r["r3"][:, 0:CA].astype(F32)
    r["dw"][:, CA:H] = vb + r["r3"][:, CA:H].astype(F32)
    rcopy(r["gx"].at[1 - xl], r["gx"].at[1 - xl], r["gs"].at[7], r["gr"].at[7], xdev).wait_recv()
    cp_gx.wait_send()
    r["dg"][...] = r["gx"][0] + r["gx"][1]
    cp_sx.wait_send()


def shards(states, injection, cotangent, gain, weight, exits, order):
    any_space = pl.BlockSpec(memory_space=pl.ANY)
    vmem = pl.BlockSpec(memory_space=pltpu.VMEM)
    smem = pl.BlockSpec(memory_space=pltpu.SMEM)
    V = pltpu.VMEM
    DMA = pltpu.SemaphoreType.DMA
    ins = dict(order=smem, exits=smem, gain=vmem, states=any_space, inj=any_space, cot=any_space, w=any_space)
    outs = dict(dinj=vmem, dw=vmem, dg=vmem)
    scratch = dict(
        st=V((2, R, D), BF16), injv=V((2, R, H), BF16), cotv=V((2, R, H), BF16), wv=V((D, H), BF16),
        stx=V((2, R, H), BF16), av=V((N, H), F32), colq=V((N, 128), F32), coli=V((N, 128), F32),
        srow=V((8, N), F32), rrow=V((8, N), F32), irow=V((8, N), F32), irx=V((8, N), F32),
        da=V((N, H), F32), dax=V((N, H), F32), db=V((N, H), BF16), dbx=V((N, H), BF16), dbl=V((N, H), BF16),
        po=V((N, H), F32), pox=V((N, H), F32), pc=V((N, H), BF16), pcx=V((N, H), BF16),
        stt=V((H, N), F32), stp=V((2, 4, 4, 96, N), BF16), p1=V((4, 4, 96, H), F32),
        pa=V((3, 4, 2, 44, CA), BF16), ra=V((3, 4, 2, 44, CA), BF16), oa=V((4, 2, 44, CA), F32),
        pb=V((3, 4, 2, 44, CB), BF16), rb=V((3, 4, 2, 44, CB), BF16), ob=V((4, 2, 44, CB), F32),
        pa2=V((3, 2, 44, CA), BF16), ra2=V((3, 2, 44, CA), BF16), oa2=V((2, 44, CA), F32),
        pb2=V((3, 2, 44, CB), BF16), rb2=V((3, 2, 44, CB), BF16), ob2=V((2, 44, CB), F32),
        p3=V((44, H), BF16), r3=V((44, H), BF16),
        gc=V((2, 1, H), F32), gz=V((4, 1, H), F32), gy=V((4, 1, H), F32), gx=V((2, 1, H), F32),
        loc=DMA((9,)), sxs=DMA, sxr=DMA, sts=DMA((2,)), str=DMA((2,)), dbs=DMA, dbr=DMA, das=DMA, dar=DMA,
        pos=DMA, por=DMA, pcs=DMA, pcr=DMA, a1s=DMA((3,)), a1r=DMA((3,)), b1s=DMA((3,)), b1r=DMA((3,)),
        a2s=DMA((3,)), a2r=DMA((3,)), b2s=DMA((3,)), b2r=DMA((3,)), x3s=DMA, x3r=DMA, gs=DMA((8,)), gr=DMA((8,)),
    )
    names = list(ins) + list(outs) + list(scratch)
    dinj, dw, dg = pl.pallas_call(
        functools.partial(kernel, names),
        out_shape=(
            jax.ShapeDtypeStruct((2, R, H), F32),
            jax.ShapeDtypeStruct((44, H), F32),
            jax.ShapeDtypeStruct((1, H), F32),
        ),
        in_specs=list(ins.values()),
        out_specs=tuple(outs.values()),
        scratch_shapes=list(scratch.values()),
        compiler_params=pltpu.CompilerParams(collective_id=0, has_side_effects=True, vmem_limit_bytes=66_000_000),
    )(order, exits, gain.reshape(1, H), states, injection, cotangent, weight)
    return dinj, dw, dg.reshape(H)


def solution(mesh):
    return jax.shard_map(
        shards,
        mesh=mesh,
        in_specs=(
            P("section", "dp", None, None),
            P("dp", None, "mp"),
            P("dp", None, "mp"),
            P("mp"),
            P(None, "mp"),
            P("dp"),
            P("dp", None),
        ),
        out_specs=(P("dp", None, "mp"), P(("section", "dp"), "mp"), P("mp")),
        check_vma=False,
    )
```

```python
import functools

import jax
import jax.numpy as jnp
from jax import lax
from jax.experimental import pallas as pl
from jax.experimental.pallas import tpu as pltpu
from jax.sharding import PartitionSpec as P

MESH = pl.DeviceIdType.MESH
F32 = jnp.float32
BF16 = jnp.bfloat16
epsilon = 1e-06

D = 2816
H = 1408
R = 128
N = 256
CW = 768
CB = H - CW
CHUNKS = ((0, 256), (256, 256), (512, 256), (768, 256), (1024, 256), (1280, 128))
RB = 32


def kernel(names, *refs):
    r = dict(zip(names, refs))
    order, exits, gain = r["order"], r["exits"], r["gain"]
    s = lax.axis_index("section")
    d = lax.axis_index("dp")
    h = lax.axis_index("mp")
    z, y, xl = d // 8, (d // 2) % 4, d % 2

    def dev(s_, z_, y_, x_, h_):
        return (s_, z_ * 8 + y_ * 2 + x_, h_)

    core = dev(1 - s, z, y, xl, h)
    part = dev(s, z, y, xl, 1 - h)
    cross = dev(1 - s, z, y, xl, 1 - h)
    xdev = dev(s, z, y, 1 - xl, h)
    xcross = dev(1 - s, z, y, 1 - xl, h)
    zdev = [dev(s, (z + t) % 4, y, xl, h) for t in (1, 2, 3)]
    ydev = [dev(s, z, (y + t) % 4, xl, h) for t in (1, 2, 3)]
    to_zero = [dev(0, (z + t) % 4, y, xl, h) for t in (1, 2, 3)]
    to_one = [dev(1, z, (y + t) % 4, xl, h) for t in (1, 2, 3)]
    ring_other = [dev(1 - s, (z + t * (1 - s)) % 4, (y + t * s) % 4, xl, h) for t in (1, 2, 3)]
    wdev = [dev(s, (z + t * s) % 4, (y + t * (1 - s)) % 4, xl, h) for t in (1, 2, 3)]
    w = y * (1 - s) + z * s

    def rcopy(src, dst, ss, rs, to):
        return pltpu.make_async_remote_copy(src, dst, ss, rs, device_id=to, device_id_type=MESH)

    swapped = order[0, 0] != 0
    first, second = exits[0], exits[1]
    exit_of = (jnp.where(swapped, second, first), jnp.where(swapped, first, second))

    def by_slot(name, j, rows, cols):
        kept = r[name][j, rows, cols].astype(F32)
        other = r[name][1 - j, rows, cols].astype(F32)
        return jnp.where(swapped, other, kept)

    loc = r["loc"]
    cp_st = [
        pltpu.make_async_copy(r["states"].at[0, j], r["st"].at[pl.ds(j * R, R)], loc.at[9 + j]) for j in range(2)
    ]
    cp_inj = pltpu.make_async_copy(r["inj"], r["injv"], loc.at[1])
    cp_cot = pltpu.make_async_copy(r["cot"], r["cotv"], loc.at[2])
    cp_w = [
        pltpu.make_async_copy(r["w"].at[:, pl.ds(c0, cw)], r["wv"].at[:, pl.ds(c0, cw)], loc.at[3 + i])
        for i, (c0, cw) in enumerate(CHUNKS)
    ]
    for c in cp_st:
        c.start()
    cp_w[0].start()
    cp_inj.start()
    for c in cp_w[1:]:
        c.start()
    cp_cot.start()

    barrier = pltpu.get_barrier_semaphore()
    everyone = [core, part, cross, xdev, xcross] + zdev + ydev + ring_other
    for p in everyone:
        pl.semaphore_signal(barrier, 1, device_id=p, device_id_type=MESH)

    for c in cp_st:
        c.wait()
    for k in range(2):
        for q in range(H // 128):
            c0 = k * H + q * 128
            r["stt"][pl.ds(q * 128, 128), :] = jnp.transpose(r["st"][:, c0 : c0 + 128].astype(F32))
        for b in range(32):
            r["stq"][k, b // 8, (b // 2) % 4, b % 2, 0:44, :] = r["stt"][b * 44 : b * 44 + 44, :].astype(BF16)

    def state_copies():
        lanes = [pl.ds(t * N, N) for t in range(4)]
        stq, mine, far = r["stq"], r["stg"].at[s], r["gts"]
        out = []
        for t in (1, 2, 3):
            out.append(
                rcopy(stq.at[:, (z + t) % 4], mine.at[..., lanes[t]], far.at[t], r["gtr"].at[s, t], to_zero[t - 1])
            )
            out.append(
                rcopy(stq.at[:, :, (y + t) % 4], mine.at[..., lanes[t]], far.at[3 + t], r["gtr"].at[s, t], to_one[t - 1])
            )
        here = (stq.at[:, z], stq.at[:, :, y])
        return out, here, mine.at[..., lanes[0]]

    def own_copies(here, into, loc_sem, send_sem, recv_sem, start):
        for k in range(2):

            @pl.when(s == k)
            def _():
                keep = pltpu.make_async_copy(here[k], into, loc_sem)
                give = rcopy(here[1 - k], into, send_sem, recv_sem, core)
                if start:
                    keep.start()
                    give.start()
                else:
                    keep.wait()
                    give.wait_send()

    cp_inj.wait()
    av = r["av"]
    st_out, st_here, st_into = state_copies()
    for i, (c0, cw) in enumerate(CHUNKS):
        cp_w[i].wait()
        if i == 3:
            pl.semaphore_wait(barrier, len(everyone))
            for c in st_out:
                c.start()
            own_copies(st_here, st_into, loc.at[0], r["gts"].at[0], r["gtr"].at[s, 0], True)
        prod = jnp.dot(r["st"][...], r["wv"][:, c0 : c0 + cw], preferred_element_type=F32)
        for j in range(2):
            inj = by_slot("injv", j, slice(None), slice(c0, c0 + cw))
            av[pl.ds(j * R, R), c0 : c0 + cw] = prod[j * R : (j + 1) * R] + inj
    cp_cot.wait()

    def lanes_sum(v):
        t = v[:, 0:128]
        for q in range(1, H // 128):
            t = t + v[:, q * 128 : (q + 1) * 128]
        return t

    def widen(v):
        return jnp.concatenate([v] * (H // 128), axis=1)

    def rowform(ref):
        return jnp.sum(jnp.transpose(ref[...]), axis=0, keepdims=True)

    def colform(row):
        return jnp.transpose(jnp.broadcast_to(row, (128, N)))

    gain_row = gain[...]

    def row_loop(step, init):
        carry = init
        for j in range(2):
            carry = lax.fori_loop(
                0,
                R // RB,
                lambda q, c, j=j: step(
                    pl.ds(pl.multiple_of(j * R + q * RB, RB), RB), j, pl.ds(pl.multiple_of(q * RB, RB), RB), c
                ),
                carry,
            )
        return carry

    def stat_step(rows, j, inner_rows, carry):
        a = av[rows, :]
        r["colq"][rows, :] = lanes_sum(a * a)
        u = by_slot("cotv", j, inner_rows, slice(None)) * gain_row
        r["coli"][rows, :] = lanes_sum(u * a)
        return carry

    row_loop(stat_step, 0)
    r["srow"][0:1, :] = rowform(r["colq"])
    r["srow"][1:2, :] = rowform(r["coli"])
    cp_stat = rcopy(r["srow"], r["rrow"], r["sts"].at[0], r["str"].at[0], part)
    cp_stat.start()

    cp_da = rcopy(r["da"], r["dax"], r["das"], r["dar"], core)
    cp_po = rcopy(r["po"], r["pox"], r["pos"], r["por"], core)
    cp_pc = rcopy(r["pc"], r["pcx"], r["pcs"], r["pcr"], cross)
    cp_in = rcopy(r["irow"], r["irx"], r["sts"].at[1], r["str"].at[1], part)

    db_into = r["dbg"].at[s]
    db_here = (r["db"].at[:, 0:CW], r["db"].at[:, CB:H])
    db_out = []
    for t in (1, 2, 3):
        rows = db_into.at[pl.ds(t * N, N)]
        db_out.append(rcopy(db_here[0], rows, r["dbs"].at[t], r["dbr"].at[s, t], to_zero[t - 1]))
        db_out.append(rcopy(db_here[1], rows, r["dbs"].at[3 + t], r["dbr"].at[s, t], to_one[t - 1]))

    def db_own(start):
        own_copies(db_here, db_into.at[pl.ds(0, N)], loc.at[11], r["dbs"].at[0], r["dbr"].at[s, 0], start)

    def send_db():
        for c in db_out:
            c.start()
        db_own(True)

    def gathered(k):
        for t in range(4):
            into_st = r["stg"].at[k, ..., pl.ds(t * N, N)]
            into_db = r["dbg"].at[k, pl.ds(t * N, N)]

            def both():
                rcopy(into_st, into_st, r["gts"].at[0], r["gtr"].at[k, t], core).wait_recv()
                rcopy(into_db, into_db, r["dbs"].at[0], r["dbr"].at[k, t], core).wait_recv()

            if t == 0:
                pl.when(s != k)(both)
            else:
                both()

    def norm_columns(sq_row, in_row):
        inv = 1.0 / jnp.sqrt(sq_row * (1.0 / D) + epsilon)
        r["colq"][...] = colform(inv)
        r["coli"][...] = colform(in_row * inv * (1.0 / D))

    def finish_da(get_c, mask_all):
        def step(rows, j, inner_rows, acc):
            inv = widen(r["colq"][rows, :])
            n = av[rows, :] * inv
            c = get_c(rows, j, inner_rows)
            da = (c * gain_row - n * widen(r["coli"][rows, :])) * inv
            g = c * n
            if mask_all:
                live = exit_of[j] > 1
                da = jnp.where(live, da, 0.0)
                g = jnp.where(live, g, 0.0)
            r["da"][rows, :] = da
            r["db"][rows, :] = da.astype(BF16)
            return acc + jnp.sum(g.reshape(RB // 8, 8, H), axis=0)

        acc = row_loop(step, jnp.zeros((8, H), F32))
        r["gc"][s] = jnp.sum(acc, axis=0, keepdims=True)

    @pl.when(s == 1)
    def _():
        cp_stat.wait_recv()
        tot = r["srow"][...] + r["rrow"][...]
        norm_columns(tot[0:1], tot[1:2])
        finish_da(lambda rows, j, ir: by_slot("cotv", j, ir, slice(None)), True)
        send_db()
        away = pl.multiple_of((1 - h) * H, 128)
        for c0, cw in CHUNKS:
            r["pc"][:, c0 : c0 + cw] = lax.dot_general(
                r["db"][...], r["wv"][pl.ds(away + c0, cw), :], (((1,), (1,)), ((), ())), preferred_element_type=F32
            ).astype(BF16)
        cp_pc.start()
        home = pl.multiple_of(h * H, 128)
        for c0, cw in CHUNKS:
            r["po"][:, c0 : c0 + cw] = lax.dot_general(
                r["db"][...], r["wv"][pl.ds(home + c0, cw), :], (((1,), (1,)), ((), ())), preferred_element_type=F32
            )
        cp_po.start()
        cp_da.start()
        cp_po.wait_send()
        cp_pc.wait_send()

    @pl.when(s == 0)
    def _():
        cp_stat.wait_recv()
        cp_po.wait_recv()
        cp_pc.wait_recv()

        def inner_step(rows, j, ir, carry):
            start = jnp.where(exit_of[j] == 1, by_slot("cotv", j, ir, slice(None)), 0.0)
            c = r["pox"][rows, :] + r["pcx"][rows, :].astype(F32) + start
            r["pox"][rows, :] = c
            r["coli"][rows, :] = lanes_sum(c * gain_row * av[rows, :])
            return carry

        row_loop(inner_step, 0)
        r["irow"][0:1, :] = rowform(r["coli"])
        cp_in.start()
        cp_in.wait()
        sq = r["srow"][0:1] + r["rrow"][0:1]
        norm_columns(sq, r["irow"][0:1] + r["irx"][0:1])
        finish_da(lambda rows, j, ir: r["pox"][rows, :], False)
        send_db()
        cp_da.start()

    cp_stat.wait_send()

    cp_gc = rcopy(r["gc"].at[s], r["gc"].at[s], r["gs"].at[0], r["gr"].at[0], core)
    cp_gc.start()

    cp_da.wait_recv()

    def inj_step(q, carry):
        tot = []
        for j in range(2):
            rows = pl.ds(pl.multiple_of(j * R + q * RB, RB), RB)
            tot.append(r["da"][rows, :] + r["dax"][rows, :])
        rows = pl.ds(pl.multiple_of(q * RB, RB), RB)
        r["dinj"][0, rows, :] = jnp.where(swapped, tot[1], tot[0])
        r["dinj"][1, rows, :] = jnp.where(swapped, tot[0], tot[1])
        return carry

    lax.fori_loop(0, R // RB, inj_step, 0)
    cp_da.wait_send()

    rcopy(r["gc"].at[1 - s], r["gc"].at[1 - s], r["gs"].at[0], r["gr"].at[0], core).wait_recv()
    cp_gc.wait_send()
    r["gz"][z] = r["gc"][0] + r["gc"][1]
    gz = [rcopy(r["gz"].at[z], r["gz"].at[z], r["gs"].at[t], r["gr"].at[t], zdev[t - 1]) for t in (1, 2, 3)]
    for c in gz:
        c.start()

    own_copies(st_here, st_into, loc.at[0], r["gts"].at[0], r["gtr"].at[s, 0], False)
    db_own(False)
    gathered(1)
    for n in range(3):
        cols = slice(n * 256, n * 256 + 256)
        r["p1"][n] = jnp.dot(
            r["stg"][1].reshape(768, 4 * N), r["dbg"][1, :, cols], preferred_element_type=F32
        ).reshape(2, 4, 2, 48, 256)
    for t in (1, 2, 3):
        zs = (z + 4 - t) % 4
        rcopy(r["gz"].at[zs], r["gz"].at[zs], r["gs"].at[t], r["gr"].at[t], zdev[t - 1]).wait_recv()
    for c in gz:
        c.wait_send()
    r["gy"][y] = r["gz"][0] + r["gz"][1] + r["gz"][2] + r["gz"][3]
    gy = [rcopy(r["gy"].at[y], r["gy"].at[y], r["gs"].at[3 + t], r["gr"].at[3 + t], ydev[t - 1]) for t in (1, 2, 3)]
    for c in gy:
        c.start()

    gathered(0)
    sends = []
    for n in range(3):
        cols = slice(n * 256, n * 256 + 256)
        v = jnp.dot(r["stg"][0].reshape(768, 4 * N), r["dbg"][0, :, cols], preferred_element_type=F32)
        v = v.reshape(2, 4, 2, 48, 256) + r["p1"][n]
        r["p1"][n] = v
        for q in range(4):
            r["pw"][n, q] = v[:, q, :, 0:44].astype(BF16)
        for t in (1, 2, 3):
            i = 3 * n + t - 1
            sends.append(
                rcopy(r["pw"].at[n, (w + t) % 4], r["rw"].at[n, t - 1], r["ws"].at[i], r["wr"].at[i], wdev[t - 1])
            )
            sends[-1].start()
    for c in st_out + db_out:
        c.wait_send()

    for t in (1, 2, 3):
        ys = (y + 4 - t) % 4
        rcopy(r["gy"].at[ys], r["gy"].at[ys], r["gs"].at[3 + t], r["gr"].at[3 + t], ydev[t - 1]).wait_recv()
    for c in gy:
        c.wait_send()
    r["gx"][xl] = r["gy"][0] + r["gy"][1] + r["gy"][2] + r["gy"][3]
    cp_gx = rcopy(r["gx"].at[xl], r["gx"].at[xl], r["gs"].at[7], r["gr"].at[7], xdev)
    cp_gx.start()

    last = []
    for n in range(3):
        for t in (1, 2, 3):
            sends[3 * n + t - 1].wait()
        v = r["p1"][n, :, w][:, :, 0:44]
        for t in range(3):
            v = v + r["rw"][n, t].astype(F32)
        r["o3"][n] = v
        r["p3"][n, 0] = r["o3"][n, s, 1 - xl].astype(BF16)
        r["p3"][n, 1] = r["o3"][n, 1 - s, 1 - xl].astype(BF16)
        last.append(rcopy(r["p3"].at[n, 0], r["r3"].at[n, 0], r["x3s"].at[3 * n], r["x3r"].at[3 * n], xdev))
        last.append(rcopy(r["p3"].at[n, 1], r["r3"].at[n, 1], r["x3s"].at[3 * n + 1], r["x3r"].at[3 * n + 1], xcross))
        last.append(rcopy(r["o3"].at[n, 1 - s, xl], r["rc"].at[n], r["x3s"].at[3 * n + 2], r["x3r"].at[3 * n + 2], core))
        for c in last[-3:]:
            c.start()
    for n in range(3):
        for c in last[3 * n : 3 * n + 3]:
            c.wait()
        own = r["o3"][n, s, xl] + r["r3"][n, 0].astype(F32)
        other = r["rc"][n] + r["r3"][n, 1].astype(F32)
        low = jnp.where(s == 0, own, other)
        high = jnp.where(s == 0, other, own)
        r["dw"][:, n * 256 : n * 256 + 256] = low
        if n == 0:
            r["dw"][:, CW : CW + 128] = high[:, 128:256]
        else:
            r["dw"][:, CB + n * 256 : CB + n * 256 + 256] = high
    rcopy(r["gx"].at[1 - xl], r["gx"].at[1 - xl], r["gs"].at[7], r["gr"].at[7], xdev).wait_recv()
    cp_gx.wait_send()
    r["dg"][...] = r["gx"][0] + r["gx"][1]


def shards(states, injection, cotangent, gain, weight, exits, order):
    any_space = pl.BlockSpec(memory_space=pl.ANY)
    vmem = pl.BlockSpec(memory_space=pltpu.VMEM)
    smem = pl.BlockSpec(memory_space=pltpu.SMEM)
    V = pltpu.VMEM
    DMA = pltpu.SemaphoreType.DMA
    ins = dict(order=smem, exits=smem, gain=vmem, states=any_space, inj=any_space, cot=any_space, w=any_space)
    outs = dict(dinj=vmem, dw=vmem, dg=vmem)
    scratch = dict(
        st=V((N, D), BF16), injv=V((2, R, H), BF16), cotv=V((2, R, H), BF16), wv=V((D, H), BF16),
        av=V((N, H), F32), colq=V((N, 128), F32), coli=V((N, 128), F32),
        srow=V((8, N), F32), rrow=V((8, N), F32), irow=V((8, N), F32), irx=V((8, N), F32),
        da=V((N, H), F32), dax=V((N, H), F32), db=V((N, H), BF16),
        po=V((N, H), F32), pox=V((N, H), F32), pc=V((N, H), BF16), pcx=V((N, H), BF16),
        stt=V((H, N), F32), stq=V((2, 4, 4, 2, 48, N), BF16), stg=V((2, 2, 4, 2, 48, 4 * N), BF16),
        dbg=V((2, 4 * N, CW), BF16), p1=V((3, 2, 4, 2, 48, 256), F32),
        pw=V((3, 4, 2, 2, 44, 256), BF16), rw=V((3, 3, 2, 2, 44, 256), BF16), o3=V((3, 2, 2, 44, 256), F32),
        p3=V((3, 2, 44, 256), BF16), r3=V((3, 2, 44, 256), BF16), rc=V((3, 44, 256), F32),
        gc=V((2, 1, H), F32), gz=V((4, 1, H), F32), gy=V((4, 1, H), F32), gx=V((2, 1, H), F32),
        loc=DMA((12,)), gts=DMA((7,)), gtr=DMA((2, 4)), dbs=DMA((7,)), dbr=DMA((2, 4)),
        sts=DMA((2,)), str=DMA((2,)), das=DMA, dar=DMA, pos=DMA, por=DMA, pcs=DMA, pcr=DMA,
        ws=DMA((9,)), wr=DMA((9,)), x3s=DMA((9,)), x3r=DMA((9,)), gs=DMA((8,)), gr=DMA((8,)),
    )
    names = list(ins) + list(outs) + list(scratch)
    dinj, dw, dg = pl.pallas_call(
        functools.partial(kernel, names),
        out_shape=(
            jax.ShapeDtypeStruct((2, R, H), F32),
            jax.ShapeDtypeStruct((44, H), F32),
            jax.ShapeDtypeStruct((1, H), F32),
        ),
        in_specs=list(ins.values()),
        out_specs=tuple(outs.values()),
        scratch_shapes=list(scratch.values()),
        compiler_params=pltpu.CompilerParams(collective_id=0, has_side_effects=True, vmem_limit_bytes=66_000_000),
    )(order, exits, gain.reshape(1, H), states, injection, cotangent, weight)
    return dinj, dw, dg.reshape(H)


def solution(mesh):
    return jax.shard_map(
        shards,
        mesh=mesh,
        in_specs=(
            P("section", "dp", None, None),
            P("dp", None, "mp"),
            P("dp", None, "mp"),
            P("mp"),
            P(None, "mp"),
            P("dp"),
            P("dp", None),
        ),
        out_specs=(P("dp", None, "mp"), P(("section", "dp"), "mp"), P("mp")),
        check_vma=False,
    )
```

```python
import functools

import jax
import jax.numpy as jnp
from jax import lax
from jax.experimental import pallas as pl
from jax.experimental.pallas import tpu as pltpu
from jax.sharding import PartitionSpec as P

MESH = pl.DeviceIdType.MESH
F32 = jnp.float32
BF16 = jnp.bfloat16
epsilon = 1e-06

D = 2816
H = 1408
R = 128
N = 256
CW = 768
CB = H - CW
WIDE = ((0, 512), (512, 512), (1024, 384))
PARTS = ((0, 512), (512, 256))
RB = 32
NEAR = {0: 0, 1: 1, 3: 2}


def depth_of(section, t):
    return 6 * N + (1 - section) * N if t == 2 else (1 - section) * 3 * N + NEAR[t] * N


def kernel(names, *refs):
    r = dict(zip(names, refs))
    order, exits, gain = r["order"], r["exits"], r["gain"]
    s = lax.axis_index("section")
    d = lax.axis_index("dp")
    h = lax.axis_index("mp")
    z, y, xl = d // 8, (d // 2) % 4, d % 2

    def dev(s_, z_, y_, x_, h_):
        return (s_, z_ * 8 + y_ * 2 + x_, h_)

    core = dev(1 - s, z, y, xl, h)
    part = dev(s, z, y, xl, 1 - h)
    cross = dev(1 - s, z, y, xl, 1 - h)
    xdev = dev(s, z, y, 1 - xl, h)
    xcross = dev(1 - s, z, y, 1 - xl, h)
    zdev = [dev(s, (z + t) % 4, y, xl, h) for t in (1, 2, 3)]
    ydev = [dev(s, z, (y + t) % 4, xl, h) for t in (1, 2, 3)]
    to_zero = [dev(0, (z + t) % 4, y, xl, h) for t in (1, 2, 3)]
    to_one = [dev(1, z, (y + t) % 4, xl, h) for t in (1, 2, 3)]
    ring_other = [dev(1 - s, (z + t * (1 - s)) % 4, (y + t * s) % 4, xl, h) for t in (1, 2, 3)]
    ring = {t: dev(s, (z + t * (1 - s)) % 4, (y + t * s) % 4, xl, h) for t in (1, 3)}
    wdev = [dev(s, (z + t * s) % 4, (y + t * (1 - s)) % 4, xl, h) for t in (1, 2, 3)]
    w = y * (1 - s) + z * s

    def rcopy(src, dst, ss, rs, to):
        return pltpu.make_async_remote_copy(src, dst, ss, rs, device_id=to, device_id_type=MESH)

    barrier = pltpu.get_barrier_semaphore()
    everyone = [core, part, cross, xdev, xcross] + zdev + ydev + ring_other
    for p in everyone:
        pl.semaphore_signal(barrier, 1, device_id=p, device_id_type=MESH)

    swapped = order[0, 0] != 0
    first, second = exits[0], exits[1]
    exit_of = (jnp.where(swapped, second, first), jnp.where(swapped, first, second))

    def by_slot(name, j, rows, cols):
        kept = r[name][j, rows, cols].astype(F32)
        other = r[name][1 - j, rows, cols].astype(F32)
        return jnp.where(swapped, other, kept)

    loc = r["loc"]
    cp_st = [
        pltpu.make_async_copy(r["states"].at[0, j], r["st"].at[pl.ds(j * R, R)], loc.at[9 + j]) for j in range(2)
    ]
    cp_inj = pltpu.make_async_copy(r["inj"], r["injv"], loc.at[1])
    cp_cot = pltpu.make_async_copy(r["cot"], r["cotv"], loc.at[2])
    cp_w = [
        pltpu.make_async_copy(r["w"].at[:, pl.ds(c0, cw)], r["wv"].at[:, pl.ds(c0, cw)], loc.at[3 + i])
        for i, (c0, cw) in enumerate(WIDE)
    ]
    for c in cp_st:
        c.start()
    cp_w[0].start()
    cp_inj.start()
    for c in cp_w[1:]:
        c.start()
    cp_cot.start()


    for c in cp_st:
        c.wait()
    for k in range(2):
        for q in range(H // 128):
            c0 = k * H + q * 128
            r["stt"][pl.ds(q * 128, 128), :] = jnp.transpose(r["st"][:, c0 : c0 + 128].astype(F32))
        for b in range(16):
            r["stq"][k, b // 4, b % 4] = r["stt"][b * 88 : b * 88 + 88, :].astype(BF16)

    def own_depth(t):
        return pl.ds(pl.multiple_of(jnp.where(s == 0, depth_of(0, t), depth_of(1, t)), N), N)

    def state_copies():
        lanes = [own_depth(t) for t in range(4)]
        stq, mine, far = r["stq"], r["stg"], r["gts"]
        out = []
        for t in (1, 2, 3):
            out.append(
                rcopy(stq.at[:, (z + t) % 4], mine.at[..., lanes[t]], far.at[t], r["gtr"].at[s, t], to_zero[t - 1])
            )
            out.append(
                rcopy(stq.at[:, :, (y + t) % 4], mine.at[..., lanes[t]], far.at[3 + t], r["gtr"].at[s, t], to_one[t - 1])
            )
        here = (stq.at[:, z], stq.at[:, :, y])
        return out, here, mine.at[..., lanes[0]]

    def own_copies(here, into, loc_sem, send_sem, recv_sem, start):
        for k in range(2):

            @pl.when(s == k)
            def _():
                keep = pltpu.make_async_copy(here[k], into, loc_sem)
                give = rcopy(here[1 - k], into, send_sem, recv_sem, core)
                if start:
                    keep.start()
                    give.start()
                else:
                    keep.wait()
                    give.wait_send()

    cp_inj.wait()
    av = r["av"]
    st_out, st_here, st_into = state_copies()
    for i, (c0, cw) in enumerate(WIDE):
        cp_w[i].wait()
        if i == 2:
            pl.semaphore_wait(barrier, len(everyone))
            for c in st_out:
                c.start()
            own_copies(st_here, st_into, loc.at[0], r["gts"].at[0], r["gtr"].at[s, 0], True)
        prod = jnp.dot(r["st"][...], r["wv"][:, c0 : c0 + cw], preferred_element_type=F32)
        for j in range(2):
            inj = by_slot("injv", j, slice(None), slice(c0, c0 + cw))
            av[pl.ds(j * R, R), c0 : c0 + cw] = prod[j * R : (j + 1) * R] + inj
    cp_cot.wait()

    def lanes_sum(v):
        t = v[:, 0:128]
        for q in range(1, H // 128):
            t = t + v[:, q * 128 : (q + 1) * 128]
        return t

    def widen(v):
        return jnp.concatenate([v] * (H // 128), axis=1)

    def rowform(ref):
        return jnp.sum(jnp.transpose(ref[...]), axis=0, keepdims=True)

    def colform(row):
        return jnp.transpose(jnp.broadcast_to(row, (128, N)))

    gain_row = gain[...].reshape(1, H)

    def row_loop(step, init):
        carry = init
        for j in range(2):
            carry = lax.fori_loop(
                0,
                R // RB,
                lambda q, c, j=j: step(
                    pl.ds(pl.multiple_of(j * R + q * RB, RB), RB), j, pl.ds(pl.multiple_of(q * RB, RB), RB), c
                ),
                carry,
            )
        return carry

    def stat_step(rows, j, inner_rows, carry):
        a = av[rows, :]
        r["colq"][rows, :] = lanes_sum(a * a)
        u = by_slot("cotv", j, inner_rows, slice(None)) * gain_row
        r["coli"][rows, :] = lanes_sum(u * a)
        return carry

    row_loop(stat_step, 0)
    r["srow"][0:1, :] = rowform(r["colq"])
    r["srow"][1:2, :] = rowform(r["coli"])
    cp_stat = rcopy(r["srow"], r["rrow"], r["sts"].at[0], r["str"].at[0], part)
    cp_stat.start()

    cp_da = rcopy(r["da"], r["dax"], r["das"], r["dar"], core)
    cp_po = rcopy(r["po"], r["pox"], r["pos"], r["por"], core)
    cp_pc = []
    for i, (c0, cw) in enumerate(WIDE):
        cols = pl.ds(c0, cw)
        cp_pc.append(rcopy(r["pc"].at[:, cols], r["pcx"].at[:, cols], r["pcs"].at[i], r["pcr"].at[i], cross))
    cp_in = rcopy(r["irow"], r["irx"], r["sts"].at[1], r["str"].at[1], part)

    db_here = (r["db"].at[:, 0:CW], r["db"].at[:, CB:H])

    def db_own(start):
        own_copies(db_here, r["dbg"].at[own_depth(0)], loc.at[11], r["dbs"], r["dbr"].at[s], start)

    db_out = {0: [], 1: []}
    relays = {}
    for k in range(2):
        for n, (c0, cw) in enumerate(PARTS):
            for i, t in enumerate((1, 3)):
                rows = r["dbg"].at[pl.ds(depth_of(k, t), N), pl.ds(c0, cw)]
                low = r["db"].at[:, pl.ds(c0, cw)]
                high = r["db"].at[:, pl.ds(CB + c0, cw)]
                arrive = r["d0r"].at[k, n, i]
                db_out[k].append(rcopy(low, rows, r["d0s"].at[n, i], arrive, to_zero[t - 1]))
                db_out[k].append(rcopy(high, rows, r["d0s"].at[n, 2 + i], arrive, to_one[t - 1]))
                half = r["dbg"].at[pl.ds(depth_of(k, t) + i * R, R), pl.ds(c0, cw)]
                into = r["dbg"].at[pl.ds(depth_of(k, 2) + i * R, R), pl.ds(c0, cw)]
                relays[k, n, i] = rcopy(half, into, r["rls"].at[k, n, i], r["d0r"].at[k, n, 2 + i], ring[t])

    def arrived(ref, sem):
        rcopy(ref, ref, r["dbs"], sem, core).wait_recv()

    def wait_states(k, ts):
        for t in ts:
            into = r["stg"].at[..., pl.ds(depth_of(k, t), N)]
            if t == 0:
                pl.when(s != k)(lambda: arrived(into, r["gtr"].at[k, 0]))
            else:
                arrived(into, r["gtr"].at[k, t])

    def wait_db_core(k):
        pl.when(s != k)(lambda: arrived(r["dbg"].at[pl.ds(depth_of(k, 0), N)], r["dbr"].at[k]))

    def relay(k, n):
        c0, cw = PARTS[n]
        for i, t in enumerate((1, 3)):
            arrived(r["dbg"].at[pl.ds(depth_of(k, t), N), pl.ds(c0, cw)], r["d0r"].at[k, n, i])
            relays[k, n, i].start()

    def wait_far(k, n):
        c0, cw = PARTS[n]
        for i in range(2):
            arrived(r["dbg"].at[pl.ds(depth_of(k, 2) + i * R, R), pl.ds(c0, cw)], r["d0r"].at[k, n, 2 + i])

    def product(d0, depth, c0, cw):
        return jnp.dot(
            r["stg"][..., d0 : d0 + depth].reshape(704, depth),
            r["dbg"][d0 : d0 + depth, c0 : c0 + cw],
            preferred_element_type=F32,
        ).reshape(2, 4, 88, cw)

    def norm_columns(sq_row, in_row):
        inv = 1.0 / jnp.sqrt(sq_row * (1.0 / D) + epsilon)
        r["colq"][...] = colform(inv)
        r["coli"][...] = colform(in_row * inv * (1.0 / D))

    def finish_da(get_c, mask_all):
        def step(rows, j, inner_rows, acc):
            inv = widen(r["colq"][rows, :])
            n = av[rows, :] * inv
            c = get_c(rows, j, inner_rows)
            da = (c * gain_row - n * widen(r["coli"][rows, :])) * inv
            g = c * n
            if mask_all:
                live = exit_of[j] > 1
                da = jnp.where(live, da, 0.0)
                g = jnp.where(live, g, 0.0)
            r["da"][rows, :] = da
            r["db"][rows, :] = da.astype(BF16)
            return acc + jnp.sum(g.reshape(RB // 8, 8, H), axis=0)

        acc = row_loop(step, jnp.zeros((8, H), F32))
        r["gc"][s] = jnp.sum(acc, axis=0, keepdims=True)

    @pl.when(s == 1)
    def _():
        cp_stat.wait_recv()
        tot = r["srow"][...] + r["rrow"][...]
        norm_columns(tot[0:1], tot[1:2])
        finish_da(lambda rows, j, ir: by_slot("cotv", j, ir, slice(None)), True)
        for c in db_out[1]:
            c.start()
        db_own(True)
        away = pl.multiple_of((1 - h) * H, 128)
        for i, (c0, cw) in enumerate(WIDE):
            r["pc"][:, c0 : c0 + cw] = lax.dot_general(
                r["db"][...], r["wv"][pl.ds(away + c0, cw), :], (((1,), (1,)), ((), ())), preferred_element_type=F32
            ).astype(BF16)
            cp_pc[i].start()
        home = pl.multiple_of(h * H, 128)
        for c0, cw in WIDE:
            r["po"][:, c0 : c0 + cw] = lax.dot_general(
                r["db"][...], r["wv"][pl.ds(home + c0, cw), :], (((1,), (1,)), ((), ())), preferred_element_type=F32
            )
        cp_po.start()
        cp_da.start()
        cp_po.wait_send()
        for c in cp_pc:
            c.wait_send()

    @pl.when(s == 0)
    def _():
        cp_stat.wait_recv()
        cp_po.wait_recv()
        for c in cp_pc:
            c.wait_recv()

        def inner_step(rows, j, ir, carry):
            start = jnp.where(exit_of[j] == 1, by_slot("cotv", j, ir, slice(None)), 0.0)
            c = r["pox"][rows, :] + r["pcx"][rows, :].astype(F32) + start
            r["pox"][rows, :] = c
            r["coli"][rows, :] = lanes_sum(c * gain_row * av[rows, :])
            return carry

        row_loop(inner_step, 0)
        r["irow"][0:1, :] = rowform(r["coli"])
        cp_in.start()
        cp_in.wait()
        sq = r["srow"][0:1] + r["rrow"][0:1]
        norm_columns(sq, r["irow"][0:1] + r["irx"][0:1])
        finish_da(lambda rows, j, ir: r["pox"][rows, :], False)
        for c in db_out[0]:
            c.start()
        db_own(True)
        cp_da.start()

    cp_stat.wait_send()

    cp_gc = rcopy(r["gc"].at[s], r["gc"].at[s], r["gs"].at[0], r["gr"].at[0], core)
    cp_gc.start()

    cp_da.wait_recv()

    def inj_step(q, carry):
        tot = []
        for j in range(2):
            rows = pl.ds(pl.multiple_of(j * R + q * RB, RB), RB)
            tot.append(r["da"][rows, :] + r["dax"][rows, :])
        rows = pl.ds(pl.multiple_of(q * RB, RB), RB)
        r["dinjv"][0, rows, :] = jnp.where(swapped, tot[1], tot[0])
        r["dinjv"][1, rows, :] = jnp.where(swapped, tot[0], tot[1])
        return carry

    lax.fori_loop(0, R // RB, inj_step, 0)
    cp_da.wait_send()
    out_inj = pltpu.make_async_copy(r["dinjv"], r["dinj"], loc.at[1])
    out_inj.start()

    rcopy(r["gc"].at[1 - s], r["gc"].at[1 - s], r["gs"].at[0], r["gr"].at[0], core).wait_recv()
    cp_gc.wait_send()
    r["gz"][z] = r["gc"][0] + r["gc"][1]
    gz = [rcopy(r["gz"].at[z], r["gz"].at[z], r["gs"].at[t], r["gr"].at[t], zdev[t - 1]) for t in (1, 2, 3)]
    for c in gz:
        c.start()

    own_copies(st_here, st_into, loc.at[0], r["gts"].at[0], r["gtr"].at[s, 0], False)
    relay(1, 0)
    relay(1, 1)
    wait_states(1, (0, 1, 3))
    wait_db_core(1)
    db_own(False)
    for c0, cw in PARTS:
        r["p1"][..., c0 : c0 + cw] = product(0, 3 * N, c0, cw)
    for t in (1, 2, 3):
        zs = (z + 4 - t) % 4
        rcopy(r["gz"].at[zs], r["gz"].at[zs], r["gs"].at[t], r["gr"].at[t], zdev[t - 1]).wait_recv()
    for c in gz:
        c.wait_send()
    r["gy"][y] = r["gz"][0] + r["gz"][1] + r["gz"][2] + r["gz"][3]
    gy = [rcopy(r["gy"].at[y], r["gy"].at[y], r["gs"].at[3 + t], r["gr"].at[3 + t], ydev[t - 1]) for t in (1, 2, 3)]
    for c in gy:
        c.start()

    wait_states(0, (0, 1, 3))
    wait_db_core(0)
    for n, (c0, cw) in enumerate(PARTS):
        relay(0, n)
        r["p1"][..., c0 : c0 + cw] = r["p1"][..., c0 : c0 + cw] + product(3 * N, 3 * N, c0, cw)

    wait_states(1, (2,))
    wait_states(0, (2,))
    sends = []
    for n, (c0, cw) in enumerate(PARTS):
        wait_far(1, n)
        wait_far(0, n)
        v = product(6 * N, 2 * N, c0, cw) + r["p1"][..., c0 : c0 + cw]
        r["p1"][..., c0 : c0 + cw] = v
        pw, rw = r["pw%d" % n], r["rw%d" % n]
        for q in range(4):
            pw[q] = v[:, q].astype(BF16)
        for t in (1, 2, 3):
            i = 3 * n + t - 1
            sends.append(rcopy(pw.at[(w + t) % 4], rw.at[t - 1], r["ws"].at[i], r["wr"].at[i], wdev[t - 1]))
            sends[-1].start()
    for c in st_out + list(relays.values()) + db_out[0]:
        c.wait_send()

    for t in (1, 2, 3):
        ys = (y + 4 - t) % 4
        rcopy(r["gy"].at[ys], r["gy"].at[ys], r["gs"].at[3 + t], r["gr"].at[3 + t], ydev[t - 1]).wait_recv()
    for c in gy:
        c.wait_send()
    r["gx"][xl] = r["gy"][0] + r["gy"][1] + r["gy"][2] + r["gy"][3]
    cp_gx = rcopy(r["gx"].at[xl], r["gx"].at[xl], r["gs"].at[7], r["gr"].at[7], xdev)
    cp_gx.start()

    last = []
    for n, (c0, cw) in enumerate(PARTS):
        for t in (1, 2, 3):
            sends[3 * n + t - 1].wait()
        v = r["p1"][:, w, :, c0 : c0 + cw]
        for t in range(3):
            v = v + r["rw%d" % n][t].astype(F32)
        o3, p3, r3, rc = (r[k + "%d" % n] for k in ("oo", "pp", "rr", "rc"))
        o3[:, 0] = v[:, 0:44]
        o3[:, 1] = v[:, 44:88]
        p3[0] = o3[s, 1 - xl].astype(BF16)
        p3[1] = o3[1 - s, 1 - xl].astype(BF16)
        last.append(rcopy(p3.at[0], r3.at[0], r["x3s"].at[3 * n], r["x3r"].at[3 * n], xdev))
        last.append(rcopy(p3.at[1], r3.at[1], r["x3s"].at[3 * n + 1], r["x3r"].at[3 * n + 1], xcross))
        last.append(rcopy(o3.at[1 - s, xl], rc, r["x3s"].at[3 * n + 2], r["x3r"].at[3 * n + 2], core))
        for c in last[-3:]:
            c.start()
    for n, (c0, cw) in enumerate(PARTS):
        for c in last[3 * n : 3 * n + 3]:
            c.wait()
        o3, r3, rc = (r[k + "%d" % n] for k in ("oo", "rr", "rc"))
        own = o3[s, xl] + r3[0].astype(F32)
        other = rc[...] + r3[1].astype(F32)
        low = jnp.where(s == 0, own, other)
        high = jnp.where(s == 0, other, own)
        skip = max(0, CW - CB - c0)
        r["dw"][:, c0 : c0 + cw] = low
        r["dw"][:, CB + c0 + skip : CB + c0 + cw] = high[:, skip:]
    rcopy(r["gx"].at[1 - xl], r["gx"].at[1 - xl], r["gs"].at[7], r["gr"].at[7], xdev).wait_recv()
    cp_gx.wait_send()
    r["dg"][...] = (r["gx"][0] + r["gx"][1]).reshape(H)
    out_inj.wait()


def finish(dinj_ref, dw_ref, dg_ref, dinj_out, dw_out, dg_out):
    dinj_out[...] = dinj_ref[...]
    dw_out[...] = dw_ref[...]
    dg_out[...] = dg_ref[...]


def shards(states, injection, cotangent, gain, weight, exits, order):
    any_space = pl.BlockSpec(memory_space=pltpu.HBM)
    vmem = pl.BlockSpec(memory_space=pltpu.VMEM)
    smem = pl.BlockSpec(memory_space=pltpu.SMEM)
    V = pltpu.VMEM
    DMA = pltpu.SemaphoreType.DMA
    ins = dict(order=smem, exits=smem, gain=vmem, states=any_space, inj=any_space, cot=any_space, w=any_space)
    outs = dict(dinj=pl.BlockSpec(memory_space=pltpu.HBM), dw=vmem, dg=vmem)
    scratch = dict(
        dinjv=V((2, R, H), F32), st=V((N, D), BF16), injv=V((2, R, H), BF16), cotv=V((2, R, H), BF16), wv=V((D, H), BF16),
        av=V((N, H), F32), colq=V((N, 128), F32), coli=V((N, 128), F32),
        srow=V((8, N), F32), rrow=V((8, N), F32), irow=V((8, N), F32), irx=V((8, N), F32),
        da=V((N, H), F32), dax=V((N, H), F32), db=V((N, H), BF16),
        po=V((N, H), F32), pox=V((N, H), F32), pc=V((N, H), BF16), pcx=V((N, H), BF16),
        stt=V((H, N), F32), stq=V((2, 4, 4, 88, N), BF16), stg=V((2, 4, 88, 8 * N), BF16),
        dbg=V((8 * N, CW), BF16), p1=V((2, 4, 88, CW), F32),
        gc=V((2, 1, H), F32), gz=V((4, 1, H), F32), gy=V((4, 1, H), F32), gx=V((2, 1, H), F32),
        d0s=DMA((2, 4)), d0r=DMA((2, 2, 4)), rls=DMA((2, 2, 2)),
        loc=DMA((12,)), gts=DMA((7,)), gtr=DMA((2, 4)), dbs=DMA, dbr=DMA((2,)),
        sts=DMA((2,)), str=DMA((2,)), das=DMA, dar=DMA, pos=DMA, por=DMA, pcs=DMA((3,)), pcr=DMA((3,)),
        ws=DMA((6,)), wr=DMA((6,)), x3s=DMA((6,)), x3r=DMA((6,)), gs=DMA((8,)), gr=DMA((8,)),
    )
    for n, (_, cw) in enumerate(PARTS):
        scratch["pw%d" % n] = V((4, 2, 88, cw), BF16)
        scratch["rw%d" % n] = V((3, 2, 88, cw), BF16)
        scratch["oo%d" % n] = V((2, 2, 44, cw), F32)
        scratch["pp%d" % n] = V((2, 44, cw), BF16)
        scratch["rr%d" % n] = V((2, 44, cw), BF16)
        scratch["rc%d" % n] = V((44, cw), F32)
    names = list(ins) + list(outs) + list(scratch)
    dinj, dw, dg = pl.pallas_call(
        functools.partial(kernel, names),
        out_shape=(
            jax.ShapeDtypeStruct((2, R, H), F32),
            jax.ShapeDtypeStruct((44, H), F32),
            jax.ShapeDtypeStruct((H,), F32),
        ),
        in_specs=list(ins.values()),
        out_specs=tuple(outs.values()),
        scratch_shapes=list(scratch.values()),
        compiler_params=pltpu.CompilerParams(collective_id=0, has_side_effects=True, vmem_limit_bytes=65_200_000),
    )(order, exits, gain, states, injection, cotangent, weight)
    return pl.pallas_call(
        finish,
        out_shape=tuple(jax.ShapeDtypeStruct(v.shape, F32) for v in (dinj, dw, dg)),
        in_specs=[vmem] * 3,
        out_specs=(vmem,) * 3,
    )(dinj, dw, dg)


def solution(mesh):
    return jax.shard_map(
        shards,
        mesh=mesh,
        in_specs=(
            P("section", "dp", None, None),
            P("dp", None, "mp"),
            P("dp", None, "mp"),
            P("mp"),
            P(None, "mp"),
            P("dp"),
            P("dp", None),
        ),
        out_specs=(P("dp", None, "mp"), P(("section", "dp"), "mp"), P("mp")),
        check_vma=False,
    )
```

```python
import functools

import jax
import jax.numpy as jnp
from jax import lax
from jax.experimental import pallas as pl
from jax.experimental.pallas import tpu as pltpu
from jax.sharding import PartitionSpec as P

MESH = pl.DeviceIdType.MESH
F32 = jnp.float32
BF16 = jnp.bfloat16
epsilon = 1e-06

D = 2816
H = 1408
R = 128
N = 256
CW = 768
CB = H - CW
WIDE = ((0, 512), (512, 512), (1024, 384))
PARTS = ((0, 512), (512, 256))
RB = 32
NEAR = {0: 0, 1: 1, 3: 2}


def depth_of(section, t):
    return 6 * N + (1 - section) * N if t == 2 else (1 - section) * 3 * N + NEAR[t] * N


def kernel(names, *refs):
    r = dict(zip(names, refs))
    order, exits, gain = r["order"], r["exits"], r["gain"]
    s = lax.axis_index("section")
    d = lax.axis_index("dp")
    h = lax.axis_index("mp")
    z, y, xl = d // 8, (d // 2) % 4, d % 2

    def dev(s_, z_, y_, x_, h_):
        return (s_, z_ * 8 + y_ * 2 + x_, h_)

    core = dev(1 - s, z, y, xl, h)
    part = dev(s, z, y, xl, 1 - h)
    cross = dev(1 - s, z, y, xl, 1 - h)
    xdev = dev(s, z, y, 1 - xl, h)
    xcross = dev(1 - s, z, y, 1 - xl, h)
    zdev = [dev(s, (z + t) % 4, y, xl, h) for t in (1, 2, 3)]
    ydev = [dev(s, z, (y + t) % 4, xl, h) for t in (1, 2, 3)]
    to_zero = [dev(0, (z + t) % 4, y, xl, h) for t in (1, 2, 3)]
    to_one = [dev(1, z, (y + t) % 4, xl, h) for t in (1, 2, 3)]
    ring_other = [dev(1 - s, (z + t * (1 - s)) % 4, (y + t * s) % 4, xl, h) for t in (1, 2, 3)]
    ring = {t: dev(s, (z + t * (1 - s)) % 4, (y + t * s) % 4, xl, h) for t in (1, 3)}
    wdev = [dev(s, (z + t * s) % 4, (y + t * (1 - s)) % 4, xl, h) for t in (1, 2, 3)]
    w = y * (1 - s) + z * s

    def rcopy(src, dst, ss, rs, to):
        return pltpu.make_async_remote_copy(src, dst, ss, rs, device_id=to, device_id_type=MESH)

    barrier = pltpu.get_barrier_semaphore()
    everyone = [core, part, cross, xdev, xcross] + zdev + ydev + ring_other
    for p in everyone:
        pl.semaphore_signal(barrier, 1, device_id=p, device_id_type=MESH)

    swapped = order[0, 0] != 0
    first, second = exits[0], exits[1]
    exit_of = (jnp.where(swapped, second, first), jnp.where(swapped, first, second))

    def by_slot(name, j, rows, cols):
        kept = r[name][j, rows, cols].astype(F32)
        other = r[name][1 - j, rows, cols].astype(F32)
        return jnp.where(swapped, other, kept)

    loc = r["loc"]
    cp_st = [
        pltpu.make_async_copy(r["states"].at[0, j], r["st"].at[pl.ds(j * R, R)], loc.at[9 + j]) for j in range(2)
    ]
    cp_inj = pltpu.make_async_copy(r["inj"], r["injv"], loc.at[1])
    cp_gain = pltpu.make_async_copy(gain, r["gainv"], loc.at[7])
    cp_cot = pltpu.make_async_copy(r["cot"], r["cotv"], loc.at[2])
    cp_w = [
        pltpu.make_async_copy(r["w"].at[:, pl.ds(c0, cw)], r["wv"].at[:, pl.ds(c0, cw)], loc.at[3 + i])
        for i, (c0, cw) in enumerate(WIDE)
    ]
    for c in cp_st:
        c.start()
    cp_w[0].start()
    cp_inj.start()
    for c in cp_w[1:]:
        c.start()
    cp_cot.start()
    cp_gain.start()


    for c in cp_st:
        c.wait()
    for k in range(2):
        for q in range(H // 128):
            c0 = k * H + q * 128
            r["stt"][pl.ds(q * 128, 128), :] = jnp.transpose(r["st"][:, c0 : c0 + 128].astype(F32))
        for b in range(16):
            r["stq"][k, b // 4, b % 4] = r["stt"][b * 88 : b * 88 + 88, :].astype(BF16)

    def own_depth(t):
        return pl.ds(pl.multiple_of(jnp.where(s == 0, depth_of(0, t), depth_of(1, t)), N), N)

    def state_copies():
        lanes = [own_depth(t) for t in range(4)]
        stq, mine, far = r["stq"], r["stg"], r["gts"]
        out = []
        for t in (1, 2, 3):
            out.append(
                rcopy(stq.at[:, (z + t) % 4], mine.at[..., lanes[t]], far.at[t], r["gtr"].at[s, t], to_zero[t - 1])
            )
            out.append(
                rcopy(stq.at[:, :, (y + t) % 4], mine.at[..., lanes[t]], far.at[3 + t], r["gtr"].at[s, t], to_one[t - 1])
            )
        here = (stq.at[:, z], stq.at[:, :, y])
        return out, here, mine.at[..., lanes[0]]

    def own_copies(here, into, loc_sem, send_sem, recv_sem, start):
        for k in range(2):

            @pl.when(s == k)
            def _():
                keep = pltpu.make_async_copy(here[k], into, loc_sem)
                give = rcopy(here[1 - k], into, send_sem, recv_sem, core)
                if start:
                    keep.start()
                    give.start()
                else:
                    keep.wait()
                    give.wait_send()

    cp_inj.wait()
    av = r["av"]
    st_out, st_here, st_into = state_copies()
    for i, (c0, cw) in enumerate(WIDE):
        cp_w[i].wait()
        if i == 2:
            pl.semaphore_wait(barrier, len(everyone))
            for c in st_out:
                c.start()
            own_copies(st_here, st_into, loc.at[0], r["gts"].at[0], r["gtr"].at[s, 0], True)
        prod = jnp.dot(r["st"][...], r["wv"][:, c0 : c0 + cw], preferred_element_type=F32)
        for j in range(2):
            inj = by_slot("injv", j, slice(None), slice(c0, c0 + cw))
            av[pl.ds(j * R, R), c0 : c0 + cw] = prod[j * R : (j + 1) * R] + inj
    cp_cot.wait()
    cp_gain.wait()

    def lanes_sum(v):
        t = v[:, 0:128]
        for q in range(1, H // 128):
            t = t + v[:, q * 128 : (q + 1) * 128]
        return t

    def widen(v):
        return jnp.concatenate([v] * (H // 128), axis=1)

    def rowform(ref):
        return jnp.sum(jnp.transpose(ref[...]), axis=0, keepdims=True)

    def colform(row):
        return jnp.transpose(jnp.broadcast_to(row, (128, N)))

    gain_row = r["gainv"][...].reshape(1, H)

    def row_loop(step, init):
        carry = init
        for j in range(2):
            carry = lax.fori_loop(
                0,
                R // RB,
                lambda q, c, j=j: step(
                    pl.ds(pl.multiple_of(j * R + q * RB, RB), RB), j, pl.ds(pl.multiple_of(q * RB, RB), RB), c
                ),
                carry,
            )
        return carry

    def stat_step(rows, j, inner_rows, carry):
        a = av[rows, :]
        r["colq"][rows, :] = lanes_sum(a * a)
        u = by_slot("cotv", j, inner_rows, slice(None)) * gain_row
        r["coli"][rows, :] = lanes_sum(u * a)
        return carry

    row_loop(stat_step, 0)
    r["srow"][0:1, :] = rowform(r["colq"])
    r["srow"][1:2, :] = rowform(r["coli"])
    cp_stat = rcopy(r["srow"], r["rrow"], r["sts"].at[0], r["str"].at[0], part)
    cp_stat.start()

    cp_da = rcopy(r["da"], r["dax"], r["das"], r["dar"], core)
    cp_po = rcopy(r["po"], r["pox"], r["pos"], r["por"], core)
    cp_pc = []
    for i, (c0, cw) in enumerate(WIDE):
        cols = pl.ds(c0, cw)
        cp_pc.append(rcopy(r["pc"].at[:, cols], r["pcx"].at[:, cols], r["pcs"].at[i], r["pcr"].at[i], cross))
    cp_in = rcopy(r["irow"], r["irx"], r["sts"].at[1], r["str"].at[1], part)

    db_here = (r["db"].at[:, 0:CW], r["db"].at[:, CB:H])

    def db_own(start):
        own_copies(db_here, r["dbg"].at[own_depth(0)], loc.at[11], r["dbs"], r["dbr"].at[s], start)

    db_out = {0: [], 1: []}
    relays = {}
    for k in range(2):
        for n, (c0, cw) in enumerate(PARTS):
            for i, t in enumerate((1, 3)):
                rows = r["dbg"].at[pl.ds(depth_of(k, t), N), pl.ds(c0, cw)]
                low = r["db"].at[:, pl.ds(c0, cw)]
                high = r["db"].at[:, pl.ds(CB + c0, cw)]
                arrive = r["d0r"].at[k, n, i]
                db_out[k].append(rcopy(low, rows, r["d0s"].at[n, i], arrive, to_zero[t - 1]))
                db_out[k].append(rcopy(high, rows, r["d0s"].at[n, 2 + i], arrive, to_one[t - 1]))
                half = r["dbg"].at[pl.ds(depth_of(k, t) + i * R, R), pl.ds(c0, cw)]
                into = r["dbg"].at[pl.ds(depth_of(k, 2) + i * R, R), pl.ds(c0, cw)]
                relays[k, n, i] = rcopy(half, into, r["rls"].at[k, n, i], r["d0r"].at[k, n, 2 + i], ring[t])

    def arrived(ref, sem):
        rcopy(ref, ref, r["dbs"], sem, core).wait_recv()

    def wait_states(k, ts):
        for t in ts:
            into = r["stg"].at[..., pl.ds(depth_of(k, t), N)]
            if t == 0:
                pl.when(s != k)(lambda: arrived(into, r["gtr"].at[k, 0]))
            else:
                arrived(into, r["gtr"].at[k, t])

    def wait_db_core(k):
        pl.when(s != k)(lambda: arrived(r["dbg"].at[pl.ds(depth_of(k, 0), N)], r["dbr"].at[k]))

    def relay(k, n):
        c0, cw = PARTS[n]
        for i, t in enumerate((1, 3)):
            arrived(r["dbg"].at[pl.ds(depth_of(k, t), N), pl.ds(c0, cw)], r["d0r"].at[k, n, i])
            relays[k, n, i].start()

    def wait_far(k, n):
        c0, cw = PARTS[n]
        for i in range(2):
            arrived(r["dbg"].at[pl.ds(depth_of(k, 2) + i * R, R), pl.ds(c0, cw)], r["d0r"].at[k, n, 2 + i])

    def product(d0, depth, c0, cw):
        return jnp.dot(
            r["stg"][..., d0 : d0 + depth].reshape(704, depth),
            r["dbg"][d0 : d0 + depth, c0 : c0 + cw],
            preferred_element_type=F32,
        ).reshape(2, 4, 88, cw)

    def norm_columns(sq_row, in_row):
        inv = 1.0 / jnp.sqrt(sq_row * (1.0 / D) + epsilon)
        r["colq"][...] = colform(inv)
        r["coli"][...] = colform(in_row * inv * (1.0 / D))

    def finish_da(get_c, mask_all):
        def step(rows, j, inner_rows, acc):
            inv = widen(r["colq"][rows, :])
            n = av[rows, :] * inv
            c = get_c(rows, j, inner_rows)
            da = (c * gain_row - n * widen(r["coli"][rows, :])) * inv
            g = c * n
            if mask_all:
                live = exit_of[j] > 1
                da = jnp.where(live, da, 0.0)
                g = jnp.where(live, g, 0.0)
            r["da"][rows, :] = da
            r["db"][rows, :] = da.astype(BF16)
            return acc + jnp.sum(g.reshape(RB // 8, 8, H), axis=0)

        acc = row_loop(step, jnp.zeros((8, H), F32))
        r["gz"][z] = jnp.sum(acc, axis=0, keepdims=True)
        for c in gz:
            c.start()

    def gathered_sum(name, sends, count, at, first, devices):
        buf = r[name]
        for t in range(1, count):
            src = (at + count - t) % count
            rcopy(buf.at[src], buf.at[src], r["gs"].at[first + t - 1], r["gr"].at[first + t - 1], devices[t - 1]).wait_recv()
        for c in sends:
            c.wait_send()
        total = buf[0]
        for t in range(1, count):
            total = total + buf[t]
        return total

    def vector_sends(name, at, first, devices):
        buf = r[name].at[at]
        return [rcopy(buf, buf, r["gs"].at[first + i], r["gr"].at[first + i], p) for i, p in enumerate(devices)]

    gz = vector_sends("gz", z, 0, zdev)
    gy = vector_sends("gy", y, 3, ydev)
    gx = vector_sends("gx", xl, 6, [xdev])
    gc = vector_sends("gc", s, 7, [core])

    @pl.when(s == 1)
    def _():
        cp_stat.wait_recv()
        tot = r["srow"][...] + r["rrow"][...]
        norm_columns(tot[0:1], tot[1:2])
        finish_da(lambda rows, j, ir: by_slot("cotv", j, ir, slice(None)), True)
        for c in db_out[1]:
            c.start()
        db_own(True)
        away = pl.multiple_of((1 - h) * H, 128)
        for i, (c0, cw) in enumerate(WIDE):
            r["pc"][:, c0 : c0 + cw] = lax.dot_general(
                r["db"][...], r["wv"][pl.ds(away + c0, cw), :], (((1,), (1,)), ((), ())), preferred_element_type=F32
            ).astype(BF16)
            cp_pc[i].start()
        home = pl.multiple_of(h * H, 128)
        for c0, cw in WIDE:
            r["po"][:, c0 : c0 + cw] = lax.dot_general(
                r["db"][...], r["wv"][pl.ds(home + c0, cw), :], (((1,), (1,)), ((), ())), preferred_element_type=F32
            )
        cp_po.start()
        cp_da.start()
        cp_po.wait_send()
        for c in cp_pc:
            c.wait_send()

    @pl.when(s == 0)
    def _():
        cp_stat.wait_recv()
        cp_po.wait_recv()
        for c in cp_pc:
            c.wait_recv()

        def inner_step(rows, j, ir, carry):
            start = jnp.where(exit_of[j] == 1, by_slot("cotv", j, ir, slice(None)), 0.0)
            c = r["pox"][rows, :] + r["pcx"][rows, :].astype(F32) + start
            r["pox"][rows, :] = c
            r["coli"][rows, :] = lanes_sum(c * gain_row * av[rows, :])
            return carry

        row_loop(inner_step, 0)
        r["irow"][0:1, :] = rowform(r["coli"])
        cp_in.start()
        cp_in.wait()
        sq = r["srow"][0:1] + r["rrow"][0:1]
        norm_columns(sq, r["irow"][0:1] + r["irx"][0:1])
        finish_da(lambda rows, j, ir: r["pox"][rows, :], False)
        for c in db_out[0]:
            c.start()
        db_own(True)
        cp_da.start()

    cp_stat.wait_send()

    own_copies(st_here, st_into, loc.at[0], r["gts"].at[0], r["gtr"].at[s, 0], False)
    relay(1, 0)
    relay(1, 1)
    wait_states(1, (0, 1, 3))
    wait_db_core(1)
    db_own(False)
    for c0, cw in PARTS:
        r["p1"][..., c0 : c0 + cw] = product(0, 3 * N, c0, cw)
    r["gy"][y] = gathered_sum("gz", gz, 4, z, 0, zdev)
    for c in gy:
        c.start()

    cp_da.wait_recv()

    def inj_step(q, carry):
        tot = []
        for j in range(2):
            rows = pl.ds(pl.multiple_of(j * R + q * RB, RB), RB)
            tot.append(r["da"][rows, :] + r["dax"][rows, :])
        rows = pl.ds(pl.multiple_of(q * RB, RB), RB)
        r["dinjv"][0, rows, :] = jnp.where(swapped, tot[1], tot[0])
        r["dinjv"][1, rows, :] = jnp.where(swapped, tot[0], tot[1])
        return carry

    lax.fori_loop(0, R // RB, inj_step, 0)
    out_inj = pltpu.make_async_copy(r["dinjv"], r["dinj"], loc.at[1])
    out_inj.start()

    wait_states(0, (0, 1, 3))
    wait_db_core(0)
    relay(0, 0)
    relay(0, 1)
    for n, (c0, cw) in enumerate(PARTS):
        r["p1"][..., c0 : c0 + cw] = r["p1"][..., c0 : c0 + cw] + product(3 * N, 3 * N, c0, cw)

    wait_states(1, (2,))
    wait_states(0, (2,))
    c0, cw = PARTS[0]
    wait_far(1, 0)
    wait_far(0, 0)
    v = product(6 * N, 2 * N, c0, cw) + r["p1"][..., c0 : c0 + cw]
    r["p1"][..., c0 : c0 + cw] = v
    for q in range(4):
        r["pw0"][q] = v[:, q].astype(BF16)
    wide = []
    for t in (1, 2, 3):
        wide.append(
            rcopy(r["pw0"].at[(w + t) % 4], r["rw0"].at[t - 1], r["ws"].at[t - 1], r["wr"].at[t - 1], wdev[t - 1])
        )
        wide[-1].start()
    c0, cw = PARTS[1]
    wait_far(1, 1)
    wait_far(0, 1)
    v = product(6 * N, 2 * N, c0, cw) + r["p1"][..., c0 : c0 + cw]
    for q in range(2):
        r["ox"][q] = v[:, :, 44 * q : 44 * q + 44]
        r["px"][q] = v[:, :, 44 * q : 44 * q + 44].astype(BF16)
    cp_x = rcopy(r["px"].at[1 - xl], r["rx"], r["x3s"].at[3], r["x3r"].at[3], xdev)
    cp_x.start()
    for c in st_out + list(relays.values()) + db_out[0] + [cp_da]:
        c.wait_send()
    r["gx"][xl] = gathered_sum("gy", gy, 4, y, 3, ydev)
    gx[0].start()

    cp_x.wait()
    v = r["ox"][xl] + r["rx"][...].astype(F32)
    r["ow"][...] = v
    for q in range(4):
        r["pw1"][q] = v[:, q].astype(BF16)
    narrow = []
    for t in (1, 2, 3):
        narrow.append(
            rcopy(r["pw1"].at[(w + t) % 4], r["rw1"].at[t - 1], r["ws"].at[2 + t], r["wr"].at[2 + t], wdev[t - 1])
        )
        narrow[-1].start()

    for c in wide:
        c.wait()
    c0, cw = PARTS[0]
    v = r["p1"][:, w, :, c0 : c0 + cw]
    for t in range(3):
        v = v + r["rw0"][t].astype(F32)
    oo0, pp0, rr0 = r["oo0"], r["pp0"], r["rr0"]
    oo0[:, 0] = v[:, 0:44]
    oo0[:, 1] = v[:, 44:88]
    pp0[0] = oo0[s, 1 - xl].astype(BF16)
    pp0[1] = oo0[1 - s, 1 - xl].astype(BF16)
    last = [
        rcopy(pp0.at[0], rr0.at[0], r["x3s"].at[0], r["x3r"].at[0], xdev),
        rcopy(pp0.at[1], rr0.at[1], r["x3s"].at[1], r["x3r"].at[1], xcross),
        rcopy(oo0.at[1 - s, xl], r["rc0"], r["x3s"].at[2], r["x3r"].at[2], core),
    ]
    for c in last:
        c.start()
    r["gc"][s] = gathered_sum("gx", gx, 2, xl, 6, [xdev])
    gc[0].start()

    for c in narrow:
        c.wait()
    v = r["ow"][:, w]
    for t in range(3):
        v = v + r["rw1"][t].astype(F32)
    r["oo1"][...] = v
    cp_rc = rcopy(r["oo1"].at[1 - s], r["rc1"], r["x3s"].at[4], r["x3r"].at[4], core)
    cp_rc.start()

    stores = []

    def put(n, own, other):
        c0, cw = PARTS[n]
        low = jnp.where(s == 0, own, other)
        high = jnp.where(s == 0, other, own)
        skip = max(0, CW - CB - c0)
        for v, first in ((low, c0), (high[:, skip:], CB + c0 + skip)):
            cols = pl.ds(first, v.shape[1])
            r["dwv"][:, cols] = v
            stores.append(pltpu.make_async_copy(r["dwv"].at[:, cols], r["dw"].at[:, cols], loc.at[3 + len(stores)]))
            stores[-1].start()

    for c in last:
        c.wait()
    put(0, oo0[s, xl] + rr0[0].astype(F32), r["rc0"][...] + rr0[1].astype(F32))
    cp_rc.wait()
    put(1, r["oo1"][s], r["rc1"][...])
    r["dgv"][...] = gathered_sum("gc", gc, 2, s, 7, [core]).reshape(H)
    stores.append(pltpu.make_async_copy(r["dgv"], r["dg"], loc.at[8]))
    stores[-1].start()
    for c in stores + [out_inj]:
        c.wait()


def finish(dinj_ref, dw_ref, dg_ref, dinj_out, dw_out, dg_out, injv, dwv, dgv, sin, sout):
    pairs = [(dw_ref, dwv, dw_out), (dg_ref, dgv, dg_out)]
    for m in range(2):
        for q in range(0, R, 64):
            rows = (m, pl.ds(q, 64))
            pairs.append((dinj_ref.at[rows], injv.at[rows], dinj_out.at[rows]))
    loads = [pltpu.make_async_copy(a, b, sin.at[i]) for i, (a, b, _) in enumerate(pairs)]
    stores = [pltpu.make_async_copy(b, c, sout.at[i]) for i, (_, b, c) in enumerate(pairs)]
    for c in loads:
        c.start()
    for a, b in zip(loads, stores):
        a.wait()
        b.start()
    for c in stores:
        c.wait()


def shards(states, injection, cotangent, gain, weight, exits, order):
    hbm = pl.BlockSpec(memory_space=pltpu.HBM)
    vmem = pl.BlockSpec(memory_space=pltpu.VMEM)
    smem = pl.BlockSpec(memory_space=pltpu.SMEM)
    V = pltpu.VMEM
    DMA = pltpu.SemaphoreType.DMA
    ins = dict(order=smem, exits=smem, gain=hbm, states=hbm, inj=hbm, cot=hbm, w=hbm)
    outs = dict(dinj=hbm, dw=hbm, dg=hbm)
    scratch = dict(
        dinjv=V((2, R, H), F32), st=V((N, D), BF16), injv=V((2, R, H), BF16), cotv=V((2, R, H), BF16), wv=V((D, H), BF16),
        av=V((N, H), F32), colq=V((N, 128), F32), coli=V((N, 128), F32),
        srow=V((8, N), F32), rrow=V((8, N), F32), irow=V((8, N), F32), irx=V((8, N), F32),
        da=V((N, H), F32), dax=V((N, H), F32), db=V((N, H), BF16),
        po=V((N, H), F32), pox=V((N, H), F32), pc=V((N, H), BF16), pcx=V((N, H), BF16),
        stt=V((H, N), F32), stq=V((2, 4, 4, 88, N), BF16), stg=V((2, 4, 88, 8 * N), BF16),
        dbg=V((8 * N, CW), BF16), p1=V((2, 4, 88, CW), F32),
        gc=V((2, 1, H), F32), gz=V((4, 1, H), F32), gy=V((4, 1, H), F32), gx=V((2, 1, H), F32),
        d0s=DMA((2, 4)), d0r=DMA((2, 2, 4)), rls=DMA((2, 2, 2)),
        loc=DMA((12,)), gts=DMA((7,)), gtr=DMA((2, 4)), dbs=DMA, dbr=DMA((2,)),
        sts=DMA((2,)), str=DMA((2,)), das=DMA, dar=DMA, pos=DMA, por=DMA, pcs=DMA((3,)), pcr=DMA((3,)),
        ws=DMA((6,)), wr=DMA((6,)), x3s=DMA((6,)), x3r=DMA((6,)), gs=DMA((8,)), gr=DMA((8,)),
    )
    wide, narrow = PARTS[0][1], PARTS[1][1]
    scratch.update(
        pw0=V((4, 2, 88, wide), BF16), rw0=V((3, 2, 88, wide), BF16), oo0=V((2, 2, 44, wide), F32),
        pp0=V((2, 44, wide), BF16), rr0=V((2, 44, wide), BF16), rc0=V((44, wide), F32),
        ox=V((2, 2, 4, 44, narrow), F32), px=V((2, 2, 4, 44, narrow), BF16), rx=V((2, 4, 44, narrow), BF16),
        ow=V((2, 4, 44, narrow), F32), pw1=V((4, 2, 44, narrow), BF16), rw1=V((3, 2, 44, narrow), BF16),
        oo1=V((2, 44, narrow), F32), rc1=V((44, narrow), F32), dwv=V((44, H), F32), dgv=V((H,), F32), gainv=V((H,), F32),
    )
    names = list(ins) + list(outs) + list(scratch)
    dinj, dw, dg = pl.pallas_call(
        functools.partial(kernel, names),
        out_shape=(
            jax.ShapeDtypeStruct((2, R, H), F32),
            jax.ShapeDtypeStruct((44, H), F32),
            jax.ShapeDtypeStruct((H,), F32),
        ),
        in_specs=list(ins.values()),
        out_specs=tuple(outs.values()),
        scratch_shapes=list(scratch.values()),
        compiler_params=pltpu.CompilerParams(collective_id=0, has_side_effects=True, vmem_limit_bytes=65_200_000),
    )(order, exits, gain, states, injection, cotangent, weight)
    return pl.pallas_call(
        finish,
        out_shape=tuple(jax.ShapeDtypeStruct(v.shape, F32) for v in (dinj, dw, dg)),
        in_specs=[hbm] * 3,
        out_specs=(hbm,) * 3,
        scratch_shapes=[V((2, R, H), F32), V((44, H), F32), V((H,), F32), DMA((6,)), DMA((6,))],
    )(dinj, dw, dg)


def solution(mesh):
    return jax.shard_map(
        shards,
        mesh=mesh,
        in_specs=(
            P("section", "dp", None, None),
            P("dp", None, "mp"),
            P("dp", None, "mp"),
            P("mp"),
            P(None, "mp"),
            P("dp"),
            P("dp", None),
        ),
        out_specs=(P("dp", None, "mp"), P(("section", "dp"), "mp"), P("mp")),
        check_vma=False,
    )
```

```python
import functools

import jax
import jax.numpy as jnp
from jax import lax
from jax.experimental import pallas as pl
from jax.experimental.pallas import tpu as pltpu
from jax.sharding import PartitionSpec as P

MESH = pl.DeviceIdType.MESH
F32 = jnp.float32
BF16 = jnp.bfloat16
epsilon = 1e-06

D = 2816
H = 1408
R = 128
N = 256
CW = 768
CB = H - CW
WIDE = ((0, 512), (512, 512), (1024, 384))
PIECES = ((0, 512), (512, 128), (640, 128))
PARTS = ((0, 512), (512, 256))
RB = 32
NEAR = {0: 0, 1: 1, 3: 2}


def depth_of(section, t):
    return 6 * N + (1 - section) * N if t == 2 else (1 - section) * 3 * N + NEAR[t] * N


def kernel(names, *refs):
    r = dict(zip(names, refs))
    order, exits, gain = r["order"], r["exits"], r["gain"]
    s = lax.axis_index("section")
    d = lax.axis_index("dp")
    h = lax.axis_index("mp")
    z, y, xl = d // 8, (d // 2) % 4, d % 2

    def dev(s_, z_, y_, x_, h_):
        return (s_, z_ * 8 + y_ * 2 + x_, h_)

    core = dev(1 - s, z, y, xl, h)
    part = dev(s, z, y, xl, 1 - h)
    cross = dev(1 - s, z, y, xl, 1 - h)
    xdev = dev(s, z, y, 1 - xl, h)
    xcross = dev(1 - s, z, y, 1 - xl, h)
    zdev = [dev(s, (z + t) % 4, y, xl, h) for t in (1, 2, 3)]
    ydev = [dev(s, z, (y + t) % 4, xl, h) for t in (1, 2, 3)]
    to_zero = [dev(0, (z + t) % 4, y, xl, h) for t in (1, 2, 3)]
    to_one = [dev(1, z, (y + t) % 4, xl, h) for t in (1, 2, 3)]
    ring_other = [dev(1 - s, (z + t * (1 - s)) % 4, (y + t * s) % 4, xl, h) for t in (1, 2, 3)]
    ring = {t: dev(s, (z + t * (1 - s)) % 4, (y + t * s) % 4, xl, h) for t in (1, 3)}
    wdev = [dev(s, (z + t * s) % 4, (y + t * (1 - s)) % 4, xl, h) for t in (1, 2, 3)]
    w = y * (1 - s) + z * s

    def rcopy(src, dst, ss, rs, to):
        return pltpu.make_async_remote_copy(src, dst, ss, rs, device_id=to, device_id_type=MESH)

    barrier = pltpu.get_barrier_semaphore()
    everyone = [core, part, cross, xdev, xcross] + zdev + ydev + ring_other
    for p in everyone:
        pl.semaphore_signal(barrier, 1, device_id=p, device_id_type=MESH)

    swapped = order[0, 0] != 0
    first, second = exits[0], exits[1]
    exit_of = (jnp.where(swapped, second, first), jnp.where(swapped, first, second))

    def by_slot(name, j, rows, cols):
        kept = r[name][j, rows, cols].astype(F32)
        other = r[name][1 - j, rows, cols].astype(F32)
        return jnp.where(swapped, other, kept)

    loc = r["loc"]
    cp_st = [
        pltpu.make_async_copy(r["states"].at[0, j], r["st"].at[pl.ds(j * R, R)], loc.at[9 + j]) for j in range(2)
    ]
    cp_inj = pltpu.make_async_copy(r["inj"], r["injv"], loc.at[1])
    cp_gain = pltpu.make_async_copy(gain, r["gainv"], loc.at[7])
    cp_cot = pltpu.make_async_copy(r["cot"], r["cotv"], loc.at[2])
    cp_w = [
        pltpu.make_async_copy(r["w"].at[:, pl.ds(c0, cw)], r["wv"].at[:, pl.ds(c0, cw)], loc.at[3 + i])
        for i, (c0, cw) in enumerate(WIDE)
    ]
    for c in cp_st:
        c.start()
    cp_w[0].start()
    cp_inj.start()
    for c in cp_w[1:]:
        c.start()
    cp_cot.start()
    cp_gain.start()


    for c in cp_st:
        c.wait()
    for k in range(2):
        for q in range(H // 128):
            c0 = k * H + q * 128
            r["stt"][pl.ds(q * 128, 128), :] = jnp.transpose(r["st"][:, c0 : c0 + 128].astype(F32))
        for b in range(16):
            r["stq"][k, b // 4, b % 4] = r["stt"][b * 88 : b * 88 + 88, :].astype(BF16)

    def own_depth(t):
        return pl.ds(pl.multiple_of(jnp.where(s == 0, depth_of(0, t), depth_of(1, t)), N), N)

    def state_copies():
        lanes = [own_depth(t) for t in range(4)]
        stq, mine, far = r["stq"], r["stg"], r["gts"]
        out = []
        for t in (1, 2, 3):
            out.append(
                rcopy(stq.at[:, (z + t) % 4], mine.at[..., lanes[t]], far.at[t], r["gtr"].at[s, t], to_zero[t - 1])
            )
            out.append(
                rcopy(stq.at[:, :, (y + t) % 4], mine.at[..., lanes[t]], far.at[3 + t], r["gtr"].at[s, t], to_one[t - 1])
            )
        here = (stq.at[:, z], stq.at[:, :, y])
        return out, here, mine.at[..., lanes[0]]

    def own_copies(here, into, loc_sem, send_sem, recv_sem, start):
        for k in range(2):

            @pl.when(s == k)
            def _():
                keep = pltpu.make_async_copy(here[k], into, loc_sem)
                give = rcopy(here[1 - k], into, send_sem, recv_sem, core)
                if start:
                    keep.start()
                    give.start()
                else:
                    keep.wait()
                    give.wait_send()

    cp_inj.wait()
    av = r["av"]
    st_out, st_here, st_into = state_copies()
    for i, (c0, cw) in enumerate(WIDE):
        cp_w[i].wait()
        if i == 2:
            pl.semaphore_wait(barrier, len(everyone))
            for c in st_out:
                c.start()
            own_copies(st_here, st_into, loc.at[0], r["gts"].at[0], r["gtr"].at[s, 0], True)
        prod = jnp.dot(r["st"][...], r["wv"][:, c0 : c0 + cw], preferred_element_type=F32)
        for j in range(2):
            inj = by_slot("injv", j, slice(None), slice(c0, c0 + cw))
            av[pl.ds(j * R, R), c0 : c0 + cw] = prod[j * R : (j + 1) * R] + inj
    cp_cot.wait()
    cp_gain.wait()

    def lanes_sum(v):
        t = v[:, 0:128]
        for q in range(1, H // 128):
            t = t + v[:, q * 128 : (q + 1) * 128]
        return t

    def widen(v):
        return jnp.concatenate([v] * (H // 128), axis=1)

    def rowform(ref):
        return jnp.sum(jnp.transpose(ref[...]), axis=0, keepdims=True)

    def colform(row):
        return jnp.transpose(jnp.broadcast_to(row, (128, N)))

    gain_row = r["gainv"][...].reshape(1, H)

    def row_loop(step, init):
        carry = init
        for j in range(2):
            carry = lax.fori_loop(
                0,
                R // RB,
                lambda q, c, j=j: step(
                    pl.ds(pl.multiple_of(j * R + q * RB, RB), RB), j, pl.ds(pl.multiple_of(q * RB, RB), RB), c
                ),
                carry,
            )
        return carry

    def stat_step(rows, j, inner_rows, carry):
        a = av[rows, :]
        r["colq"][rows, :] = lanes_sum(a * a)
        u = by_slot("cotv", j, inner_rows, slice(None)) * gain_row
        r["coli"][rows, :] = lanes_sum(u * a)
        return carry

    row_loop(stat_step, 0)
    r["srow"][0:1, :] = rowform(r["colq"])
    r["srow"][1:2, :] = rowform(r["coli"])
    cp_stat = rcopy(r["srow"], r["rrow"], r["sts"].at[0], r["str"].at[0], part)
    cp_stat.start()

    cp_da = rcopy(r["da"], r["dax"], r["das"], r["dar"], core)
    cp_po = rcopy(r["po"], r["pox"], r["pos"], r["por"], core)
    cp_pc = []
    for i, (c0, cw) in enumerate(WIDE):
        cols = pl.ds(c0, cw)
        cp_pc.append(rcopy(r["pc"].at[:, cols], r["pcx"].at[:, cols], r["pcs"].at[i], r["pcr"].at[i], cross))
    cp_in = rcopy(r["irow"], r["irx"], r["sts"].at[1], r["str"].at[1], part)

    db_here = (r["db"].at[:, 0:CW], r["db"].at[:, CB:H])

    def db_own(start):
        own_copies(db_here, r["dbg"].at[own_depth(0)], loc.at[11], r["dbs"], r["dbr"].at[s], start)

    db_out = {0: [], 1: []}
    relays = {}
    for k in range(2):
        for n, (c0, cw) in enumerate(PIECES):
            for i, t in enumerate((1, 3)):
                rows = r["dbg"].at[pl.ds(depth_of(k, t), N), pl.ds(c0, cw)]
                low = r["db"].at[:, pl.ds(c0, cw)]
                high = r["db"].at[:, pl.ds(CB + c0, cw)]
                arrive = r["d0r"].at[k, n, i]
                if c0 < CB:
                    db_out[k].append(rcopy(low, rows, r["d0s"].at[n, i], arrive, to_zero[t - 1]))
                db_out[k].append(rcopy(high, rows, r["d0s"].at[n, 2 + i], arrive, to_one[t - 1]))
                half = r["dbg"].at[pl.ds(depth_of(k, t) + i * R, R), pl.ds(c0, cw)]
                into = r["dbg"].at[pl.ds(depth_of(k, 2) + i * R, R), pl.ds(c0, cw)]
                relays[k, n, i] = rcopy(half, into, r["rls"].at[k, n, i], r["d0r"].at[k, n, 2 + i], ring[t])

    def arrived(ref, sem):
        rcopy(ref, ref, r["dbs"], sem, core).wait_recv()

    def wait_states(k, ts):
        for t in ts:
            into = r["stg"].at[..., pl.ds(depth_of(k, t), N)]
            if t == 0:
                pl.when(s != k)(lambda: arrived(into, r["gtr"].at[k, 0]))
            else:
                arrived(into, r["gtr"].at[k, t])

    def wait_db_core(k):
        pl.when(s != k)(lambda: arrived(r["dbg"].at[pl.ds(depth_of(k, 0), N)], r["dbr"].at[k]))

    def each_piece(part, act):
        if part == 0:
            act(0)
        else:
            act(1)
            pl.when(s == 1)(lambda: act(2))

    def relay(k, part):
        def act(n):
            c0, cw = PIECES[n]
            for i, t in enumerate((1, 3)):
                arrived(r["dbg"].at[pl.ds(depth_of(k, t), N), pl.ds(c0, cw)], r["d0r"].at[k, n, i])
                relays[k, n, i].start()

        each_piece(part, act)

    def wait_far(k, part):
        def act(n):
            c0, cw = PIECES[n]
            for i in range(2):
                arrived(r["dbg"].at[pl.ds(depth_of(k, 2) + i * R, R), pl.ds(c0, cw)], r["d0r"].at[k, n, 2 + i])

        each_piece(part, act)

    def product(d0, depth, c0, cw):
        return jnp.dot(
            r["stg"][..., d0 : d0 + depth].reshape(704, depth),
            r["dbg"][d0 : d0 + depth, c0 : c0 + cw],
            preferred_element_type=F32,
        ).reshape(2, 4, 88, cw)

    def norm_columns(sq_row, in_row):
        inv = 1.0 / jnp.sqrt(sq_row * (1.0 / D) + epsilon)
        r["colq"][...] = colform(inv)
        r["coli"][...] = colform(in_row * inv * (1.0 / D))

    def finish_da(get_c, mask_all):
        def step(rows, j, inner_rows, acc):
            inv = widen(r["colq"][rows, :])
            n = av[rows, :] * inv
            c = get_c(rows, j, inner_rows)
            da = (c * gain_row - n * widen(r["coli"][rows, :])) * inv
            g = c * n
            if mask_all:
                live = exit_of[j] > 1
                da = jnp.where(live, da, 0.0)
                g = jnp.where(live, g, 0.0)
            r["da"][rows, :] = da
            r["db"][rows, :] = da.astype(BF16)
            return acc + jnp.sum(g.reshape(RB // 8, 8, H), axis=0)

        acc = row_loop(step, jnp.zeros((8, H), F32))
        r["gz"][z] = jnp.sum(acc, axis=0, keepdims=True)
        for c in gz:
            c.start()

    def gathered_sum(name, sends, count, at, first, devices):
        buf = r[name]
        for t in range(1, count):
            src = (at + count - t) % count
            rcopy(buf.at[src], buf.at[src], r["gs"].at[first + t - 1], r["gr"].at[first + t - 1], devices[t - 1]).wait_recv()
        for c in sends:
            c.wait_send()
        total = buf[0]
        for t in range(1, count):
            total = total + buf[t]
        return total

    def vector_sends(name, at, first, devices):
        buf = r[name].at[at]
        return [rcopy(buf, buf, r["gs"].at[first + i], r["gr"].at[first + i], p) for i, p in enumerate(devices)]

    gz = vector_sends("gz", z, 0, zdev)
    gy = vector_sends("gy", y, 3, ydev)
    gx = vector_sends("gx", xl, 6, [xdev])
    gc = vector_sends("gc", s, 7, [core])

    @pl.when(s == 1)
    def _():
        cp_stat.wait_recv()
        tot = r["srow"][...] + r["rrow"][...]
        norm_columns(tot[0:1], tot[1:2])
        finish_da(lambda rows, j, ir: by_slot("cotv", j, ir, slice(None)), True)
        for c in db_out[1]:
            c.start()
        db_own(True)
        away = pl.multiple_of((1 - h) * H, 128)
        for i, (c0, cw) in enumerate(WIDE):
            r["pc"][:, c0 : c0 + cw] = lax.dot_general(
                r["db"][...], r["wv"][pl.ds(away + c0, cw), :], (((1,), (1,)), ((), ())), preferred_element_type=F32
            ).astype(BF16)
            cp_pc[i].start()
        home = pl.multiple_of(h * H, 128)
        for c0, cw in WIDE:
            r["po"][:, c0 : c0 + cw] = lax.dot_general(
                r["db"][...], r["wv"][pl.ds(home + c0, cw), :], (((1,), (1,)), ((), ())), preferred_element_type=F32
            )
        cp_po.start()
        cp_po.wait_send()
        for c in cp_pc:
            c.wait_send()

    @pl.when(s == 0)
    def _():
        cp_stat.wait_recv()
        cp_po.wait_recv()
        for c in cp_pc:
            c.wait_recv()

        def inner_step(rows, j, ir, carry):
            start = jnp.where(exit_of[j] == 1, by_slot("cotv", j, ir, slice(None)), 0.0)
            c = r["pox"][rows, :] + r["pcx"][rows, :].astype(F32) + start
            r["pox"][rows, :] = c
            r["coli"][rows, :] = lanes_sum(c * gain_row * av[rows, :])
            return carry

        row_loop(inner_step, 0)
        r["irow"][0:1, :] = rowform(r["coli"])
        cp_in.start()
        cp_in.wait()
        sq = r["srow"][0:1] + r["rrow"][0:1]
        norm_columns(sq, r["irow"][0:1] + r["irx"][0:1])
        finish_da(lambda rows, j, ir: r["pox"][rows, :], False)
        for c in db_out[0]:
            c.start()
        db_own(True)

    cp_stat.wait_send()

    own_copies(st_here, st_into, loc.at[0], r["gts"].at[0], r["gtr"].at[s, 0], False)
    relay(1, 0)
    relay(1, 1)
    wait_states(1, (0, 1, 3))
    wait_db_core(1)
    db_own(False)
    for c0, cw in PARTS:
        r["p1"][..., c0 : c0 + cw] = product(0, 3 * N, c0, cw)
    r["gy"][y] = gathered_sum("gz", gz, 4, z, 0, zdev)
    for c in gy:
        c.start()

    wait_states(0, (0, 1, 3))
    wait_db_core(0)
    relay(0, 0)
    relay(0, 1)
    cp_da.start()
    for n, (c0, cw) in enumerate(PARTS):
        r["p1"][..., c0 : c0 + cw] = r["p1"][..., c0 : c0 + cw] + product(3 * N, 3 * N, c0, cw)

    wait_states(1, (2,))
    wait_states(0, (2,))
    c0, cw = PARTS[0]
    wait_far(1, 0)
    wait_far(0, 0)
    v = product(6 * N, 2 * N, c0, cw) + r["p1"][..., c0 : c0 + cw]
    r["p1"][..., c0 : c0 + cw] = v
    for q in range(4):
        r["pw0"][q] = v[:, q].astype(BF16)
    wide = []
    for t in (1, 2, 3):
        wide.append(
            rcopy(r["pw0"].at[(w + t) % 4], r["rw0"].at[t - 1], r["ws"].at[t - 1], r["wr"].at[t - 1], wdev[t - 1])
        )
        wide[-1].start()
    c0, cw = PARTS[1]
    wait_far(1, 1)
    wait_far(0, 1)
    v = product(6 * N, 2 * N, c0, cw) + r["p1"][..., c0 : c0 + cw]
    for q in range(2):
        r["ox"][q] = v[:, :, 44 * q : 44 * q + 44]
        r["px"][q] = v[:, :, 44 * q : 44 * q + 44].astype(BF16)
    cp_x = rcopy(r["px"].at[1 - xl], r["rx"], r["x3s"].at[3], r["x3r"].at[3], xdev)
    cp_x.start()
    cp_da.wait_recv()

    def inj_step(q, carry):
        tot = []
        for j in range(2):
            rows = pl.ds(pl.multiple_of(j * R + q * RB, RB), RB)
            tot.append(r["da"][rows, :] + r["dax"][rows, :])
        rows = pl.ds(pl.multiple_of(q * RB, RB), RB)
        r["dinjv"][0, rows, :] = jnp.where(swapped, tot[1], tot[0])
        r["dinjv"][1, rows, :] = jnp.where(swapped, tot[0], tot[1])
        return carry

    lax.fori_loop(0, R // RB, inj_step, 0)
    out_inj = pltpu.make_async_copy(r["dinjv"], r["dinj"], loc.at[1])
    out_inj.start()

    for c in st_out + db_out[0] + [cp_da]:
        c.wait_send()

    def relays_sent(n):
        for k in range(2):
            for i in range(2):
                relays[k, n, i].wait_send()

    each_piece(0, relays_sent)
    each_piece(1, relays_sent)
    r["gx"][xl] = gathered_sum("gy", gy, 4, y, 3, ydev)
    gx[0].start()

    cp_x.wait()
    v = r["ox"][xl] + r["rx"][...].astype(F32)
    r["ow"][...] = v
    for q in range(4):
        r["pw1"][q] = v[:, q].astype(BF16)
    narrow = []
    for t in (1, 2, 3):
        narrow.append(
            rcopy(r["pw1"].at[(w + t) % 4], r["rw1"].at[t - 1], r["ws"].at[2 + t], r["wr"].at[2 + t], wdev[t - 1])
        )
        narrow[-1].start()

    for c in wide:
        c.wait()
    c0, cw = PARTS[0]
    v = r["p1"][:, w, :, c0 : c0 + cw]
    for t in range(3):
        v = v + r["rw0"][t].astype(F32)
    oo0, pp0, rr0 = r["oo0"], r["pp0"], r["rr0"]
    oo0[:, 0] = v[:, 0:44]
    oo0[:, 1] = v[:, 44:88]
    pp0[0] = oo0[s, 1 - xl].astype(BF16)
    pp0[1] = oo0[1 - s, 1 - xl].astype(BF16)
    last = [
        rcopy(pp0.at[0], rr0.at[0], r["x3s"].at[0], r["x3r"].at[0], xdev),
        rcopy(pp0.at[1], rr0.at[1], r["x3s"].at[1], r["x3r"].at[1], xcross),
        rcopy(oo0.at[1 - s, xl], r["rc0"], r["x3s"].at[2], r["x3r"].at[2], core),
    ]
    for c in last:
        c.start()
    r["gc"][s] = gathered_sum("gx", gx, 2, xl, 6, [xdev])
    gc[0].start()

    for c in narrow:
        c.wait()
    v = r["ow"][:, w]
    for t in range(3):
        v = v + r["rw1"][t].astype(F32)
    r["oo1"][...] = v
    cp_rc = rcopy(r["oo1"].at[1 - s], r["rc1"], r["x3s"].at[4], r["x3r"].at[4], core)
    cp_rc.start()

    stores = []

    def put(n, own, other):
        c0, cw = PARTS[n]
        low = jnp.where(s == 0, own, other)
        high = jnp.where(s == 0, other, own)
        kept = min(cw, CB - c0)
        for v, first in ((low[:, :kept], c0), (high, CB + c0)):
            cols = pl.ds(first, v.shape[1])
            r["dwv"][:, cols] = v
            stores.append(pltpu.make_async_copy(r["dwv"].at[:, cols], r["dw"].at[:, cols], loc.at[3 + len(stores)]))
            stores[-1].start()

    for c in last:
        c.wait()
    put(0, oo0[s, xl] + rr0[0].astype(F32), r["rc0"][...] + rr0[1].astype(F32))
    cp_rc.wait()
    put(1, r["oo1"][s], r["rc1"][...])
    r["dgv"][...] = gathered_sum("gc", gc, 2, s, 7, [core]).reshape(H)
    stores.append(pltpu.make_async_copy(r["dgv"], r["dg"], loc.at[8]))
    stores[-1].start()
    for c in stores + [out_inj]:
        c.wait()


def finish(dinj_ref, dw_ref, dg_ref, dinj_out, dw_out, dg_out, injv, dwv, dgv, sin, sout):
    pairs = [(dw_ref, dwv, dw_out), (dg_ref, dgv, dg_out)]
    for m in range(2):
        for q in range(0, R, 64):
            rows = (m, pl.ds(q, 64))
            pairs.append((dinj_ref.at[rows], injv.at[rows], dinj_out.at[rows]))
    loads = [pltpu.make_async_copy(a, b, sin.at[i]) for i, (a, b, _) in enumerate(pairs)]
    stores = [pltpu.make_async_copy(b, c, sout.at[i]) for i, (_, b, c) in enumerate(pairs)]
    for c in loads:
        c.start()
    for a, b in zip(loads, stores):
        a.wait()
        b.start()
    for c in stores:
        c.wait()


def shards(states, injection, cotangent, gain, weight, exits, order):
    hbm = pl.BlockSpec(memory_space=pltpu.HBM)
    vmem = pl.BlockSpec(memory_space=pltpu.VMEM)
    smem = pl.BlockSpec(memory_space=pltpu.SMEM)
    V = pltpu.VMEM
    DMA = pltpu.SemaphoreType.DMA
    ins = dict(order=smem, exits=smem, gain=hbm, states=hbm, inj=hbm, cot=hbm, w=hbm)
    outs = dict(dinj=hbm, dw=hbm, dg=hbm)
    scratch = dict(
        dinjv=V((2, R, H), F32), st=V((N, D), BF16), injv=V((2, R, H), BF16), cotv=V((2, R, H), BF16), wv=V((D, H), BF16),
        av=V((N, H), F32), colq=V((N, 128), F32), coli=V((N, 128), F32),
        srow=V((8, N), F32), rrow=V((8, N), F32), irow=V((8, N), F32), irx=V((8, N), F32),
        da=V((N, H), F32), dax=V((N, H), F32), db=V((N, H), BF16),
        po=V((N, H), F32), pox=V((N, H), F32), pc=V((N, H), BF16), pcx=V((N, H), BF16),
        stt=V((H, N), F32), stq=V((2, 4, 4, 88, N), BF16), stg=V((2, 4, 88, 8 * N), BF16),
        dbg=V((8 * N, CW), BF16), p1=V((2, 4, 88, CW), F32),
        gc=V((2, 1, H), F32), gz=V((4, 1, H), F32), gy=V((4, 1, H), F32), gx=V((2, 1, H), F32),
        d0s=DMA((3, 4)), d0r=DMA((2, 3, 4)), rls=DMA((2, 3, 2)),
        loc=DMA((12,)), gts=DMA((7,)), gtr=DMA((2, 4)), dbs=DMA, dbr=DMA((2,)),
        sts=DMA((2,)), str=DMA((2,)), das=DMA, dar=DMA, pos=DMA, por=DMA, pcs=DMA((3,)), pcr=DMA((3,)),
        ws=DMA((6,)), wr=DMA((6,)), x3s=DMA((6,)), x3r=DMA((6,)), gs=DMA((8,)), gr=DMA((8,)),
    )
    wide, narrow = PARTS[0][1], PARTS[1][1]
    scratch.update(
        pw0=V((4, 2, 88, wide), BF16), rw0=V((3, 2, 88, wide), BF16), oo0=V((2, 2, 44, wide), F32),
        pp0=V((2, 44, wide), BF16), rr0=V((2, 44, wide), BF16), rc0=V((44, wide), F32),
        ox=V((2, 2, 4, 44, narrow), F32), px=V((2, 2, 4, 44, narrow), BF16), rx=V((2, 4, 44, narrow), BF16),
        ow=V((2, 4, 44, narrow), F32), pw1=V((4, 2, 44, narrow), BF16), rw1=V((3, 2, 44, narrow), BF16),
        oo1=V((2, 44, narrow), F32), rc1=V((44, narrow), F32), dwv=V((44, H), F32), dgv=V((H,), F32), gainv=V((H,), F32),
    )
    names = list(ins) + list(outs) + list(scratch)
    dinj, dw, dg = pl.pallas_call(
        functools.partial(kernel, names),
        out_shape=(
            jax.ShapeDtypeStruct((2, R, H), F32),
            jax.ShapeDtypeStruct((44, H), F32),
            jax.ShapeDtypeStruct((H,), F32),
        ),
        in_specs=list(ins.values()),
        out_specs=tuple(outs.values()),
        scratch_shapes=list(scratch.values()),
        compiler_params=pltpu.CompilerParams(collective_id=0, has_side_effects=True, vmem_limit_bytes=65_200_000),
    )(order, exits, gain, states, injection, cotangent, weight)
    return pl.pallas_call(
        finish,
        out_shape=tuple(jax.ShapeDtypeStruct(v.shape, F32) for v in (dinj, dw, dg)),
        in_specs=[hbm] * 3,
        out_specs=(hbm,) * 3,
        scratch_shapes=[V((2, R, H), F32), V((44, H), F32), V((H,), F32), DMA((6,)), DMA((6,))],
    )(dinj, dw, dg)


def solution(mesh):
    return jax.shard_map(
        shards,
        mesh=mesh,
        in_specs=(
            P("section", "dp", None, None),
            P("dp", None, "mp"),
            P("dp", None, "mp"),
            P("mp"),
            P(None, "mp"),
            P("dp"),
            P("dp", None),
        ),
        out_specs=(P("dp", None, "mp"), P(("section", "dp"), "mp"), P("mp")),
        check_vma=False,
    )
```

```python
import functools

import jax
import jax.numpy as jnp
from jax import lax
from jax.experimental import pallas as pl
from jax.experimental.pallas import tpu as pltpu
from jax.sharding import PartitionSpec as P

MESH = pl.DeviceIdType.MESH
F32 = jnp.float32
BF16 = jnp.bfloat16
epsilon = 1e-06

D = 2816
H = 1408
R = 128
N = 256
CW = 768
CB = H - CW
WIDE = ((0, 512), (512, 512), (1024, 384))
PIECES = ((0, 512), (512, 128), (640, 128))
PARTS = ((0, 512), (512, 256))
RB = 32
NEAR = {0: 0, 1: 1, 3: 2}


def depth_of(section, t):
    return 6 * N + (1 - section) * N if t == 2 else (1 - section) * 3 * N + NEAR[t] * N


def kernel(names, *refs):
    r = dict(zip(names, refs))
    order, exits, gain = r["order"], r["exits"], r["gain"]
    s = lax.axis_index("section")
    d = lax.axis_index("dp")
    h = lax.axis_index("mp")
    z, y, xl = d // 8, (d // 2) % 4, d % 2

    def dev(s_, z_, y_, x_, h_):
        return (s_, z_ * 8 + y_ * 2 + x_, h_)

    core = dev(1 - s, z, y, xl, h)
    part = dev(s, z, y, xl, 1 - h)
    cross = dev(1 - s, z, y, xl, 1 - h)
    xdev = dev(s, z, y, 1 - xl, h)
    xcross = dev(1 - s, z, y, 1 - xl, h)
    zdev = [dev(s, (z + t) % 4, y, xl, h) for t in (1, 2, 3)]
    ydev = [dev(s, z, (y + t) % 4, xl, h) for t in (1, 2, 3)]
    to_zero = [dev(0, (z + t) % 4, y, xl, h) for t in (1, 2, 3)]
    to_one = [dev(1, z, (y + t) % 4, xl, h) for t in (1, 2, 3)]
    ring_other = [dev(1 - s, (z + t * (1 - s)) % 4, (y + t * s) % 4, xl, h) for t in (1, 2, 3)]
    ring = {t: dev(s, (z + t * (1 - s)) % 4, (y + t * s) % 4, xl, h) for t in (1, 3)}
    wdev = [dev(s, (z + t * s) % 4, (y + t * (1 - s)) % 4, xl, h) for t in (1, 2, 3)]
    w = y * (1 - s) + z * s

    def rcopy(src, dst, ss, rs, to):
        return pltpu.make_async_remote_copy(src, dst, ss, rs, device_id=to, device_id_type=MESH)

    barrier = pltpu.get_barrier_semaphore()
    everyone = [core, part, cross, xdev, xcross] + zdev + ydev + ring_other
    for p in everyone:
        pl.semaphore_signal(barrier, 1, device_id=p, device_id_type=MESH)

    swapped = order[0, 0] != 0
    first, second = exits[0], exits[1]
    exit_of = (jnp.where(swapped, second, first), jnp.where(swapped, first, second))

    def by_slot(name, j, rows, cols):
        kept = r[name][j, rows, cols].astype(F32)
        other = r[name][1 - j, rows, cols].astype(F32)
        return jnp.where(swapped, other, kept)

    loc = r["loc"]
    cp_st = [
        pltpu.make_async_copy(r["states"].at[0, j], r["st"].at[pl.ds(j * R, R)], loc.at[9 + j]) for j in range(2)
    ]
    cp_inj = pltpu.make_async_copy(r["inj"], r["injv"], loc.at[1])
    cp_gain = pltpu.make_async_copy(gain, r["gainv"], loc.at[7])
    cp_cot = pltpu.make_async_copy(r["cot"], r["cotv"], loc.at[2])
    cp_w = [
        pltpu.make_async_copy(r["w"].at[:, pl.ds(c0, cw)], r["wv"].at[:, pl.ds(c0, cw)], loc.at[3 + i])
        for i, (c0, cw) in enumerate(WIDE)
    ]
    for c in cp_st:
        c.start()
    cp_w[0].start()
    cp_inj.start()
    for c in cp_w[1:]:
        c.start()
    cp_cot.start()
    cp_gain.start()


    for c in cp_st:
        c.wait()
    for k in range(2):
        for q in range(H // 128):
            c0 = k * H + q * 128
            r["stt"][pl.ds(q * 128, 128), :] = jnp.transpose(r["st"][:, c0 : c0 + 128].astype(F32))
        for b in range(16):
            r["stq"][k, b // 4, b % 4] = r["stt"][b * 88 : b * 88 + 88, :].astype(BF16)

    def own_depth(t):
        return pl.ds(pl.multiple_of(jnp.where(s == 0, depth_of(0, t), depth_of(1, t)), N), N)

    def state_copies():
        lanes = [own_depth(t) for t in range(4)]
        stq, mine, far = r["stq"], r["stg"], r["gts"]
        out = []
        for t in (1, 2, 3):
            out.append(
                rcopy(stq.at[:, (z + t) % 4], mine.at[..., lanes[t]], far.at[t], r["gtr"].at[s, t], to_zero[t - 1])
            )
            out.append(
                rcopy(stq.at[:, :, (y + t) % 4], mine.at[..., lanes[t]], far.at[3 + t], r["gtr"].at[s, t], to_one[t - 1])
            )
        here = (stq.at[:, z], stq.at[:, :, y])
        return out, here, mine.at[..., lanes[0]]

    def own_copies(here, into, loc_sem, send_sem, recv_sem, start):
        for k in range(2):

            @pl.when(s == k)
            def _():
                keep = pltpu.make_async_copy(here[k], into, loc_sem)
                give = rcopy(here[1 - k], into, send_sem, recv_sem, core)
                if start:
                    keep.start()
                    give.start()
                else:
                    keep.wait()
                    give.wait_send()

    cp_inj.wait()
    av = r["av"]
    st_out, st_here, st_into = state_copies()
    for i, (c0, cw) in enumerate(WIDE):
        cp_w[i].wait()
        if i == 2:
            pl.semaphore_wait(barrier, len(everyone))
            for c in st_out:
                c.start()
            own_copies(st_here, st_into, loc.at[0], r["gts"].at[0], r["gtr"].at[s, 0], True)
        prod = jnp.dot(r["st"][...], r["wv"][:, c0 : c0 + cw], preferred_element_type=F32)
        for j in range(2):
            inj = by_slot("injv", j, slice(None), slice(c0, c0 + cw))
            av[pl.ds(j * R, R), c0 : c0 + cw] = prod[j * R : (j + 1) * R] + inj
    cp_cot.wait()
    cp_gain.wait()

    def lanes_sum(v):
        t = v[:, 0:128]
        for q in range(1, H // 128):
            t = t + v[:, q * 128 : (q + 1) * 128]
        return t

    def widen(v):
        return jnp.concatenate([v] * (H // 128), axis=1)

    def rowform(ref):
        return jnp.sum(jnp.transpose(ref[...]), axis=0, keepdims=True)

    def colform(row):
        return jnp.transpose(jnp.broadcast_to(row, (128, N)))

    gain_row = r["gainv"][...].reshape(1, H)

    def row_loop(step, init):
        carry = init
        for j in range(2):
            carry = lax.fori_loop(
                0,
                R // RB,
                lambda q, c, j=j: step(
                    pl.ds(pl.multiple_of(j * R + q * RB, RB), RB), j, pl.ds(pl.multiple_of(q * RB, RB), RB), c
                ),
                carry,
            )
        return carry

    def stat_step(rows, j, inner_rows, carry):
        a = av[rows, :]
        r["colq"][rows, :] = lanes_sum(a * a)
        u = by_slot("cotv", j, inner_rows, slice(None)) * gain_row
        r["coli"][rows, :] = lanes_sum(u * a)
        return carry

    row_loop(stat_step, 0)
    r["srow"][0:1, :] = rowform(r["colq"])
    r["srow"][1:2, :] = rowform(r["coli"])
    cp_stat = rcopy(r["srow"], r["rrow"], r["sts"].at[0], r["str"].at[0], part)
    cp_stat.start()

    cp_da = rcopy(r["da"], r["dax"], r["das"], r["dar"], core)
    cp_po = rcopy(r["po"], r["pox"], r["pos"], r["por"], core)
    cp_pc = []
    for i, (c0, cw) in enumerate(WIDE):
        cols = pl.ds(c0, cw)
        cp_pc.append(rcopy(r["pc"].at[:, cols], r["pcx"].at[:, cols], r["pcs"].at[i], r["pcr"].at[i], cross))
    cp_in = rcopy(r["irow"], r["irx"], r["sts"].at[1], r["str"].at[1], part)

    db_here = (r["db"].at[:, 0:CW], r["db"].at[:, CB:H])

    def db_own(start):
        own_copies(db_here, r["dbg"].at[own_depth(0)], loc.at[11], r["dbs"], r["dbr"].at[s], start)

    db_out = {0: [], 1: []}
    relays = {}
    for k in range(2):
        for n, (c0, cw) in enumerate(PIECES):
            for i, t in enumerate((1, 3)):
                rows = r["dbg"].at[pl.ds(depth_of(k, t), N), pl.ds(c0, cw)]
                low = r["db"].at[:, pl.ds(c0, cw)]
                high = r["db"].at[:, pl.ds(CB + c0, cw)]
                arrive = r["d0r"].at[k, n, i]
                if c0 < CB:
                    db_out[k].append(rcopy(low, rows, r["d0s"].at[n, i], arrive, to_zero[t - 1]))
                db_out[k].append(rcopy(high, rows, r["d0s"].at[n, 2 + i], arrive, to_one[t - 1]))
                half = r["dbg"].at[pl.ds(depth_of(k, t) + i * R, R), pl.ds(c0, cw)]
                into = r["dbg"].at[pl.ds(depth_of(k, 2) + i * R, R), pl.ds(c0, cw)]
                relays[k, n, i] = rcopy(half, into, r["rls"].at[k, n, i], r["d0r"].at[k, n, 2 + i], ring[t])

    def arrived(ref, sem):
        rcopy(ref, ref, r["dbs"], sem, core).wait_recv()

    def wait_states(k, ts):
        for t in ts:
            into = r["stg"].at[..., pl.ds(depth_of(k, t), N)]
            if t == 0:
                pl.when(s != k)(lambda: arrived(into, r["gtr"].at[k, 0]))
            else:
                arrived(into, r["gtr"].at[k, t])

    def wait_db_core(k):
        pl.when(s != k)(lambda: arrived(r["dbg"].at[pl.ds(depth_of(k, 0), N)], r["dbr"].at[k]))

    def each_piece(part, act):
        if part == 0:
            act(0)
        else:
            act(1)
            pl.when(s == 1)(lambda: act(2))

    def relay(k, part):
        def act(n):
            c0, cw = PIECES[n]
            for i, t in enumerate((1, 3)):
                arrived(r["dbg"].at[pl.ds(depth_of(k, t), N), pl.ds(c0, cw)], r["d0r"].at[k, n, i])
                relays[k, n, i].start()

        each_piece(part, act)

    def wait_far(k, part):
        def act(n):
            c0, cw = PIECES[n]
            for i in range(2):
                arrived(r["dbg"].at[pl.ds(depth_of(k, 2) + i * R, R), pl.ds(c0, cw)], r["d0r"].at[k, n, 2 + i])

        each_piece(part, act)

    def product(d0, depth, c0, cw):
        return jnp.dot(
            r["stg"][..., d0 : d0 + depth].reshape(704, depth),
            r["dbg"][d0 : d0 + depth, c0 : c0 + cw],
            preferred_element_type=F32,
        ).reshape(2, 4, 88, cw)

    def norm_columns(sq_row, in_row):
        inv = 1.0 / jnp.sqrt(sq_row * (1.0 / D) + epsilon)
        r["colq"][...] = colform(inv)
        r["coli"][...] = colform(in_row * inv * (1.0 / D))

    def finish_da(get_c, mask_all):
        def step(rows, j, inner_rows, acc):
            inv = widen(r["colq"][rows, :])
            n = av[rows, :] * inv
            c = get_c(rows, j, inner_rows)
            da = (c * gain_row - n * widen(r["coli"][rows, :])) * inv
            g = c * n
            if mask_all:
                live = exit_of[j] > 1
                da = jnp.where(live, da, 0.0)
                g = jnp.where(live, g, 0.0)
            r["da"][rows, :] = da
            r["db"][rows, :] = da.astype(BF16)
            return acc + jnp.sum(g.reshape(RB // 8, 8, H), axis=0)

        acc = row_loop(step, jnp.zeros((8, H), F32))
        r["gz"][z] = jnp.sum(acc, axis=0, keepdims=True)
        for c in gz:
            c.start()

    def gathered_sum(name, sends, count, at, first, devices):
        buf = r[name]
        for t in range(1, count):
            src = (at + count - t) % count
            rcopy(buf.at[src], buf.at[src], r["gs"].at[first + t - 1], r["gr"].at[first + t - 1], devices[t - 1]).wait_recv()
        for c in sends:
            c.wait_send()
        total = buf[0]
        for t in range(1, count):
            total = total + buf[t]
        return total

    def vector_sends(name, at, first, devices):
        buf = r[name].at[at]
        return [rcopy(buf, buf, r["gs"].at[first + i], r["gr"].at[first + i], p) for i, p in enumerate(devices)]

    gz = vector_sends("gz", z, 0, zdev)
    gy = vector_sends("gy", y, 3, ydev)
    gx = vector_sends("gx", xl, 6, [xdev])
    gc = vector_sends("gc", s, 7, [core])

    @pl.when(s == 1)
    def _():
        cp_stat.wait_recv()
        tot = r["srow"][...] + r["rrow"][...]
        norm_columns(tot[0:1], tot[1:2])
        finish_da(lambda rows, j, ir: by_slot("cotv", j, ir, slice(None)), True)
        for c in db_out[1]:
            c.start()
        db_own(True)
        away = pl.multiple_of((1 - h) * H, 128)
        for i, (c0, cw) in enumerate(WIDE):
            r["pc"][:, c0 : c0 + cw] = lax.dot_general(
                r["db"][...], r["wv"][pl.ds(away + c0, cw), :], (((1,), (1,)), ((), ())), preferred_element_type=F32
            ).astype(BF16)
            cp_pc[i].start()
        home = pl.multiple_of(h * H, 128)
        for c0, cw in WIDE:
            r["po"][:, c0 : c0 + cw] = lax.dot_general(
                r["db"][...], r["wv"][pl.ds(home + c0, cw), :], (((1,), (1,)), ((), ())), preferred_element_type=F32
            )
        cp_po.start()
        cp_po.wait_send()
        for c in cp_pc:
            c.wait_send()

    @pl.when(s == 0)
    def _():
        cp_stat.wait_recv()
        cp_po.wait_recv()
        for c in cp_pc:
            c.wait_recv()

        def inner_step(rows, j, ir, carry):
            start = jnp.where(exit_of[j] == 1, by_slot("cotv", j, ir, slice(None)), 0.0)
            c = r["pox"][rows, :] + r["pcx"][rows, :].astype(F32) + start
            r["pox"][rows, :] = c
            r["coli"][rows, :] = lanes_sum(c * gain_row * av[rows, :])
            return carry

        row_loop(inner_step, 0)
        r["irow"][0:1, :] = rowform(r["coli"])
        cp_in.start()
        cp_in.wait()
        sq = r["srow"][0:1] + r["rrow"][0:1]
        norm_columns(sq, r["irow"][0:1] + r["irx"][0:1])
        finish_da(lambda rows, j, ir: r["pox"][rows, :], False)
        for c in db_out[0]:
            c.start()
        db_own(True)

    cp_stat.wait_send()

    own_copies(st_here, st_into, loc.at[0], r["gts"].at[0], r["gtr"].at[s, 0], False)
    relay(1, 0)
    relay(1, 1)
    wait_states(1, (0, 1, 3))
    wait_db_core(1)
    db_own(False)
    for c0, cw in PARTS:
        r["p1"][..., c0 : c0 + cw] = product(0, 3 * N, c0, cw)
    r["gy"][y] = gathered_sum("gz", gz, 4, z, 0, zdev)
    for c in gy:
        c.start()

    wait_states(0, (0, 1, 3))
    wait_db_core(0)
    relay(0, 0)
    relay(0, 1)
    for n, (c0, cw) in enumerate(PARTS):
        r["p1"][..., c0 : c0 + cw] = r["p1"][..., c0 : c0 + cw] + product(3 * N, 3 * N, c0, cw)

    wait_states(1, (2,))
    wait_states(0, (2,))
    c0, cw = PARTS[0]
    wait_far(1, 0)
    wait_far(0, 0)
    v = product(6 * N, 2 * N, c0, cw) + r["p1"][..., c0 : c0 + cw]
    r["p1"][..., c0 : c0 + cw] = v
    for q in range(4):
        r["pw0"][q] = v[:, q].astype(BF16)
    wide = []
    for t in (1, 2, 3):
        wide.append(
            rcopy(r["pw0"].at[(w + t) % 4], r["rw0"].at[t - 1], r["ws"].at[t - 1], r["wr"].at[t - 1], wdev[t - 1])
        )
        wide[-1].start()
    c0, cw = PARTS[1]
    wait_far(1, 1)
    wait_far(0, 1)
    v = product(6 * N, 2 * N, c0, cw) + r["p1"][..., c0 : c0 + cw]
    for q in range(2):
        r["ox"][q] = v[:, :, 44 * q : 44 * q + 44]
        r["px"][q] = v[:, :, 44 * q : 44 * q + 44].astype(BF16)
    cp_x = rcopy(r["px"].at[1 - xl], r["rx"], r["x3s"].at[3], r["x3r"].at[3], xdev)
    cp_x.start()
    cp_da.start()
    cp_da.wait_recv()

    def inj_step(q, carry):
        tot = []
        for j in range(2):
            rows = pl.ds(pl.multiple_of(j * R + q * RB, RB), RB)
            tot.append(r["da"][rows, :] + r["dax"][rows, :])
        rows = pl.ds(pl.multiple_of(q * RB, RB), RB)
        r["dinjv"][0, rows, :] = jnp.where(swapped, tot[1], tot[0])
        r["dinjv"][1, rows, :] = jnp.where(swapped, tot[0], tot[1])
        return carry

    lax.fori_loop(0, R // RB, inj_step, 0)
    out_inj = pltpu.make_async_copy(r["dinjv"], r["dinj"], loc.at[1])
    out_inj.start()

    cp_x.wait()
    v = r["ox"][xl] + r["rx"][...].astype(F32)
    r["ow"][...] = v
    for q in range(4):
        r["pw1"][q] = v[:, q].astype(BF16)
    narrow = []
    for t in (1, 2, 3):
        narrow.append(
            rcopy(r["pw1"].at[(w + t) % 4], r["rw1"].at[t - 1], r["ws"].at[2 + t], r["wr"].at[2 + t], wdev[t - 1])
        )
        narrow[-1].start()

    for c in st_out + db_out[0] + [cp_da]:
        c.wait_send()

    def relays_sent(n):
        for k in range(2):
            for i in range(2):
                relays[k, n, i].wait_send()

    each_piece(0, relays_sent)
    each_piece(1, relays_sent)
    r["gx"][xl] = gathered_sum("gy", gy, 4, y, 3, ydev)
    gx[0].start()

    for c in wide:
        c.wait()
    c0, cw = PARTS[0]
    v = r["p1"][:, w, :, c0 : c0 + cw]
    for t in range(3):
        v = v + r["rw0"][t].astype(F32)
    oo0, pp0, rr0 = r["oo0"], r["pp0"], r["rr0"]
    oo0[:, 0] = v[:, 0:44]
    oo0[:, 1] = v[:, 44:88]
    pp0[0] = oo0[s, 1 - xl].astype(BF16)
    pp0[1] = oo0[1 - s, 1 - xl].astype(BF16)
    last = [
        rcopy(pp0.at[0], rr0.at[0], r["x3s"].at[0], r["x3r"].at[0], xdev),
        rcopy(pp0.at[1], rr0.at[1], r["x3s"].at[1], r["x3r"].at[1], xcross),
        rcopy(oo0.at[1 - s, xl], r["rc0"], r["x3s"].at[2], r["x3r"].at[2], core),
    ]
    for c in last:
        c.start()
    r["gc"][s] = gathered_sum("gx", gx, 2, xl, 6, [xdev])
    gc[0].start()

    for c in narrow:
        c.wait()
    v = r["ow"][:, w]
    for t in range(3):
        v = v + r["rw1"][t].astype(F32)
    r["oo1"][...] = v
    cp_rc = rcopy(r["oo1"].at[1 - s], r["rc1"], r["x3s"].at[4], r["x3r"].at[4], core)
    cp_rc.start()

    stores = []

    def put(n, own, other):
        c0, cw = PARTS[n]
        low = jnp.where(s == 0, own, other)
        high = jnp.where(s == 0, other, own)
        kept = min(cw, CB - c0)
        for v, first in ((low[:, :kept], c0), (high, CB + c0)):
            cols = pl.ds(first, v.shape[1])
            r["dwv"][:, cols] = v
            stores.append(pltpu.make_async_copy(r["dwv"].at[:, cols], r["dw"].at[:, cols], loc.at[3 + len(stores)]))
            stores[-1].start()

    for c in last:
        c.wait()
    put(0, oo0[s, xl] + rr0[0].astype(F32), r["rc0"][...] + rr0[1].astype(F32))
    cp_rc.wait()
    put(1, r["oo1"][s], r["rc1"][...])
    r["dgv"][...] = gathered_sum("gc", gc, 2, s, 7, [core]).reshape(H)
    stores.append(pltpu.make_async_copy(r["dgv"], r["dg"], loc.at[8]))
    stores[-1].start()
    for c in stores + [out_inj]:
        c.wait()


def finish(dinj_ref, dw_ref, dg_ref, dinj_out, dw_out, dg_out, injv, dwv, dgv, sin, sout):
    pairs = [(dw_ref, dwv, dw_out), (dg_ref, dgv, dg_out)]
    for m in range(2):
        for q in range(0, R, 64):
            rows = (m, pl.ds(q, 64))
            pairs.append((dinj_ref.at[rows], injv.at[rows], dinj_out.at[rows]))
    loads = [pltpu.make_async_copy(a, b, sin.at[i]) for i, (a, b, _) in enumerate(pairs)]
    stores = [pltpu.make_async_copy(b, c, sout.at[i]) for i, (_, b, c) in enumerate(pairs)]
    for c in loads:
        c.start()
    for a, b in zip(loads, stores):
        a.wait()
        b.start()
    for c in stores:
        c.wait()


def shards(states, injection, cotangent, gain, weight, exits, order):
    hbm = pl.BlockSpec(memory_space=pltpu.HBM)
    vmem = pl.BlockSpec(memory_space=pltpu.VMEM)
    smem = pl.BlockSpec(memory_space=pltpu.SMEM)
    V = pltpu.VMEM
    DMA = pltpu.SemaphoreType.DMA
    ins = dict(order=smem, exits=smem, gain=hbm, states=hbm, inj=hbm, cot=hbm, w=hbm)
    outs = dict(dinj=hbm, dw=hbm, dg=hbm)
    scratch = dict(
        dinjv=V((2, R, H), F32), st=V((N, D), BF16), injv=V((2, R, H), BF16), cotv=V((2, R, H), BF16), wv=V((D, H), BF16),
        av=V((N, H), F32), colq=V((N, 128), F32), coli=V((N, 128), F32),
        srow=V((8, N), F32), rrow=V((8, N), F32), irow=V((8, N), F32), irx=V((8, N), F32),
        da=V((N, H), F32), dax=V((N, H), F32), db=V((N, H), BF16),
        po=V((N, H), F32), pox=V((N, H), F32), pc=V((N, H), BF16), pcx=V((N, H), BF16),
        stt=V((H, N), F32), stq=V((2, 4, 4, 88, N), BF16), stg=V((2, 4, 88, 8 * N), BF16),
        dbg=V((8 * N, CW), BF16), p1=V((2, 4, 88, CW), F32),
        gc=V((2, 1, H), F32), gz=V((4, 1, H), F32), gy=V((4, 1, H), F32), gx=V((2, 1, H), F32),
        d0s=DMA((3, 4)), d0r=DMA((2, 3, 4)), rls=DMA((2, 3, 2)),
        loc=DMA((12,)), gts=DMA((7,)), gtr=DMA((2, 4)), dbs=DMA, dbr=DMA((2,)),
        sts=DMA((2,)), str=DMA((2,)), das=DMA, dar=DMA, pos=DMA, por=DMA, pcs=DMA((3,)), pcr=DMA((3,)),
        ws=DMA((6,)), wr=DMA((6,)), x3s=DMA((6,)), x3r=DMA((6,)), gs=DMA((8,)), gr=DMA((8,)),
    )
    wide, narrow = PARTS[0][1], PARTS[1][1]
    scratch.update(
        pw0=V((4, 2, 88, wide), BF16), rw0=V((3, 2, 88, wide), BF16), oo0=V((2, 2, 44, wide), F32),
        pp0=V((2, 44, wide), BF16), rr0=V((2, 44, wide), BF16), rc0=V((44, wide), F32),
        ox=V((2, 2, 4, 44, narrow), F32), px=V((2, 2, 4, 44, narrow), BF16), rx=V((2, 4, 44, narrow), BF16),
        ow=V((2, 4, 44, narrow), F32), pw1=V((4, 2, 44, narrow), BF16), rw1=V((3, 2, 44, narrow), BF16),
        oo1=V((2, 44, narrow), F32), rc1=V((44, narrow), F32), dwv=V((44, H), F32), dgv=V((H,), F32), gainv=V((H,), F32),
    )
    names = list(ins) + list(outs) + list(scratch)
    dinj, dw, dg = pl.pallas_call(
        functools.partial(kernel, names),
        out_shape=(
            jax.ShapeDtypeStruct((2, R, H), F32),
            jax.ShapeDtypeStruct((44, H), F32),
            jax.ShapeDtypeStruct((H,), F32),
        ),
        in_specs=list(ins.values()),
        out_specs=tuple(outs.values()),
        scratch_shapes=list(scratch.values()),
        compiler_params=pltpu.CompilerParams(collective_id=0, has_side_effects=True, vmem_limit_bytes=65_200_000),
    )(order, exits, gain, states, injection, cotangent, weight)
    return pl.pallas_call(
        finish,
        out_shape=tuple(jax.ShapeDtypeStruct(v.shape, F32) for v in (dinj, dw, dg)),
        in_specs=[hbm] * 3,
        out_specs=(hbm,) * 3,
        scratch_shapes=[V((2, R, H), F32), V((44, H), F32), V((H,), F32), DMA((6,)), DMA((6,))],
    )(dinj, dw, dg)


def solution(mesh):
    return jax.shard_map(
        shards,
        mesh=mesh,
        in_specs=(
            P("section", "dp", None, None),
            P("dp", None, "mp"),
            P("dp", None, "mp"),
            P("mp"),
            P(None, "mp"),
            P("dp"),
            P("dp", None),
        ),
        out_specs=(P("dp", None, "mp"), P(("section", "dp"), "mp"), P("mp")),
        check_vma=False,
    )
```

```python
import functools

import jax
import jax.numpy as jnp
from jax import lax
from jax.experimental import pallas as pl
from jax.experimental.pallas import tpu as pltpu
from jax.sharding import PartitionSpec as P

MESH = pl.DeviceIdType.MESH
F32 = jnp.float32
BF16 = jnp.bfloat16
epsilon = 1e-06

D = 2816
H = 1408
R = 128
N = 256
CW = 768
CB = H - CW
WIDE = ((0, 512), (512, 512), (1024, 384))
PIECES = ((0, 512), (512, 128), (640, 128))
PARTS = ((0, 512), (512, 256))
RB = 32
NEAR = {0: 0, 1: 1, 3: 2}


def depth_of(section, t):
    return 6 * N + (1 - section) * N if t == 2 else (1 - section) * 3 * N + NEAR[t] * N


def kernel(names, *refs):
    r = dict(zip(names, refs))
    order, exits, gain = r["order"], r["exits"], r["gain"]
    s = lax.axis_index("section")
    d = lax.axis_index("dp")
    h = lax.axis_index("mp")
    z, y, xl = d // 8, (d // 2) % 4, d % 2

    def dev(s_, z_, y_, x_, h_):
        return (s_, z_ * 8 + y_ * 2 + x_, h_)

    core = dev(1 - s, z, y, xl, h)
    part = dev(s, z, y, xl, 1 - h)
    cross = dev(1 - s, z, y, xl, 1 - h)
    xdev = dev(s, z, y, 1 - xl, h)
    xcross = dev(1 - s, z, y, 1 - xl, h)
    zdev = [dev(s, (z + t) % 4, y, xl, h) for t in (1, 2, 3)]
    ydev = [dev(s, z, (y + t) % 4, xl, h) for t in (1, 2, 3)]
    to_zero = [dev(0, (z + t) % 4, y, xl, h) for t in (1, 2, 3)]
    to_one = [dev(1, z, (y + t) % 4, xl, h) for t in (1, 2, 3)]
    ring_other = [dev(1 - s, (z + t * (1 - s)) % 4, (y + t * s) % 4, xl, h) for t in (1, 2, 3)]
    ring = {t: dev(s, (z + t * (1 - s)) % 4, (y + t * s) % 4, xl, h) for t in (1, 3)}
    wdev = [dev(s, (z + t * s) % 4, (y + t * (1 - s)) % 4, xl, h) for t in (1, 2, 3)]
    w = y * (1 - s) + z * s

    def rcopy(src, dst, ss, rs, to):
        return pltpu.make_async_remote_copy(src, dst, ss, rs, device_id=to, device_id_type=MESH)

    barrier = pltpu.get_barrier_semaphore()
    everyone = [core, part, cross, xdev, xcross] + zdev + ydev + ring_other
    for p in everyone:
        pl.semaphore_signal(barrier, 1, device_id=p, device_id_type=MESH)

    swapped = order[0, 0] != 0
    first, second = exits[0], exits[1]
    exit_of = (jnp.where(swapped, second, first), jnp.where(swapped, first, second))

    def by_slot(name, j, rows, cols):
        kept = r[name][j, rows, cols].astype(F32)
        other = r[name][1 - j, rows, cols].astype(F32)
        return jnp.where(swapped, other, kept)

    loc = r["loc"]
    cp_st = [
        pltpu.make_async_copy(r["states"].at[0, j], r["st"].at[pl.ds(j * R, R)], loc.at[9 + j]) for j in range(2)
    ]
    cp_inj = pltpu.make_async_copy(r["inj"], r["injv"], loc.at[1])
    cp_gain = pltpu.make_async_copy(gain, r["gainv"], loc.at[7])
    cp_cot = pltpu.make_async_copy(r["cot"], r["cotv"], loc.at[2])
    cp_w = [
        pltpu.make_async_copy(r["w"].at[:, pl.ds(c0, cw)], r["wv"].at[:, pl.ds(c0, cw)], loc.at[3 + i])
        for i, (c0, cw) in enumerate(WIDE)
    ]
    for c in cp_st:
        c.start()
    cp_w[0].start()
    cp_inj.start()
    for c in cp_w[1:]:
        c.start()
    cp_cot.start()
    cp_gain.start()


    for c in cp_st:
        c.wait()
    for k in range(2):
        for q in range(H // 128):
            c0 = k * H + q * 128
            r["stt"][pl.ds(q * 128, 128), :] = jnp.transpose(r["st"][:, c0 : c0 + 128].astype(F32))
        for b in range(16):
            r["stq"][k, b // 4, b % 4] = r["stt"][b * 88 : b * 88 + 88, :].astype(BF16)

    def own_depth(t):
        return pl.ds(pl.multiple_of(jnp.where(s == 0, depth_of(0, t), depth_of(1, t)), N), N)

    def state_copies():
        lanes = [own_depth(t) for t in range(4)]
        stq, mine, far = r["stq"], r["stg"], r["gts"]
        out = []
        for t in (1, 2, 3):
            out.append(
                rcopy(stq.at[:, (z + t) % 4], mine.at[..., lanes[t]], far.at[t], r["gtr"].at[s, t], to_zero[t - 1])
            )
            out.append(
                rcopy(stq.at[:, :, (y + t) % 4], mine.at[..., lanes[t]], far.at[3 + t], r["gtr"].at[s, t], to_one[t - 1])
            )
        here = (stq.at[:, z], stq.at[:, :, y])
        return out, here, mine.at[..., lanes[0]]

    def own_copies(here, into, loc_sem, send_sem, recv_sem, start):
        for k in range(2):

            @pl.when(s == k)
            def _():
                keep = pltpu.make_async_copy(here[k], into, loc_sem)
                give = rcopy(here[1 - k], into, send_sem, recv_sem, core)
                if start:
                    keep.start()
                    give.start()
                else:
                    keep.wait()
                    give.wait_send()

    cp_inj.wait()
    av = r["av"]
    st_out, st_here, st_into = state_copies()
    for i, (c0, cw) in enumerate(WIDE):
        cp_w[i].wait()
        if i == 2:
            pl.semaphore_wait(barrier, len(everyone))
            for c in st_out:
                c.start()
            own_copies(st_here, st_into, loc.at[0], r["gts"].at[0], r["gtr"].at[s, 0], True)
        prod = jnp.dot(r["st"][...], r["wv"][:, c0 : c0 + cw], preferred_element_type=F32)
        for j in range(2):
            inj = by_slot("injv", j, slice(None), slice(c0, c0 + cw))
            av[pl.ds(j * R, R), c0 : c0 + cw] = prod[j * R : (j + 1) * R] + inj
    cp_cot.wait()
    cp_gain.wait()

    def lanes_sum(v):
        t = v[:, 0:128]
        for q in range(1, H // 128):
            t = t + v[:, q * 128 : (q + 1) * 128]
        return t

    def widen(v):
        return jnp.concatenate([v] * (H // 128), axis=1)

    def rowform(ref):
        return jnp.sum(jnp.transpose(ref[...]), axis=0, keepdims=True)

    def colform(row):
        return jnp.transpose(jnp.broadcast_to(row, (128, N)))

    gain_row = r["gainv"][...].reshape(1, H)

    def row_loop(step, init):
        carry = init
        for j in range(2):
            carry = lax.fori_loop(
                0,
                R // RB,
                lambda q, c, j=j: step(
                    pl.ds(pl.multiple_of(j * R + q * RB, RB), RB), j, pl.ds(pl.multiple_of(q * RB, RB), RB), c
                ),
                carry,
            )
        return carry

    def stat_step(rows, j, inner_rows, carry):
        a = av[rows, :]
        r["colq"][rows, :] = lanes_sum(a * a)
        u = by_slot("cotv", j, inner_rows, slice(None)) * gain_row
        r["coli"][rows, :] = lanes_sum(u * a)
        return carry

    row_loop(stat_step, 0)
    r["srow"][0:1, :] = rowform(r["colq"])
    r["srow"][1:2, :] = rowform(r["coli"])
    cp_stat = rcopy(r["srow"], r["rrow"], r["sts"].at[0], r["str"].at[0], part)
    cp_stat.start()

    cp_da = rcopy(r["da"], r["dax"], r["das"], r["dar"], core)
    cp_po = rcopy(r["po"], r["pox"], r["pos"], r["por"], core)
    cp_pc = []
    for i, (c0, cw) in enumerate(WIDE):
        cols = pl.ds(c0, cw)
        cp_pc.append(rcopy(r["pc"].at[:, cols], r["pcx"].at[:, cols], r["pcs"].at[i], r["pcr"].at[i], cross))
    cp_in = rcopy(r["irow"], r["irx"], r["sts"].at[1], r["str"].at[1], part)

    db_here = (r["db"].at[:, 0:CW], r["db"].at[:, CB:H])

    def db_own(start):
        own_copies(db_here, r["dbg"].at[own_depth(0)], loc.at[11], r["dbs"], r["dbr"].at[s], start)

    db_out = {0: [], 1: []}
    relays = {}
    for k in range(2):
        for n, (c0, cw) in enumerate(PIECES):
            for i, t in enumerate((1, 3)):
                rows = r["dbg"].at[pl.ds(depth_of(k, t), N), pl.ds(c0, cw)]
                low = r["db"].at[:, pl.ds(c0, cw)]
                high = r["db"].at[:, pl.ds(CB + c0, cw)]
                arrive = r["d0r"].at[k, n, i]
                if c0 < CB:
                    db_out[k].append(rcopy(low, rows, r["d0s"].at[n, i], arrive, to_zero[t - 1]))
                db_out[k].append(rcopy(high, rows, r["d0s"].at[n, 2 + i], arrive, to_one[t - 1]))
                half = r["dbg"].at[pl.ds(depth_of(k, t) + i * R, R), pl.ds(c0, cw)]
                into = r["dbg"].at[pl.ds(depth_of(k, 2) + i * R, R), pl.ds(c0, cw)]
                relays[k, n, i] = rcopy(half, into, r["rls"].at[k, n, i], r["d0r"].at[k, n, 2 + i], ring[t])

    def arrived(ref, sem):
        rcopy(ref, ref, r["dbs"], sem, core).wait_recv()

    def wait_states(k, ts):
        for t in ts:
            into = r["stg"].at[..., pl.ds(depth_of(k, t), N)]
            if t == 0:
                pl.when(s != k)(lambda: arrived(into, r["gtr"].at[k, 0]))
            else:
                arrived(into, r["gtr"].at[k, t])

    def wait_db_core(k):
        pl.when(s != k)(lambda: arrived(r["dbg"].at[pl.ds(depth_of(k, 0), N)], r["dbr"].at[k]))

    def each_piece(part, act):
        if part == 0:
            act(0)
        else:
            act(1)
            pl.when(s == 1)(lambda: act(2))

    def relay(k, part):
        def act(n):
            c0, cw = PIECES[n]
            for i, t in enumerate((1, 3)):
                arrived(r["dbg"].at[pl.ds(depth_of(k, t), N), pl.ds(c0, cw)], r["d0r"].at[k, n, i])
                relays[k, n, i].start()

        each_piece(part, act)

    def wait_far(k, part):
        def act(n):
            c0, cw = PIECES[n]
            for i in range(2):
                arrived(r["dbg"].at[pl.ds(depth_of(k, 2) + i * R, R), pl.ds(c0, cw)], r["d0r"].at[k, n, 2 + i])

        each_piece(part, act)

    def product(d0, depth, c0, cw):
        return jnp.dot(
            r["stg"][..., d0 : d0 + depth].reshape(704, depth),
            r["dbg"][d0 : d0 + depth, c0 : c0 + cw],
            preferred_element_type=F32,
        ).reshape(2, 4, 88, cw)

    def norm_columns(sq_row, in_row):
        inv = 1.0 / jnp.sqrt(sq_row * (1.0 / D) + epsilon)
        r["colq"][...] = colform(inv)
        r["coli"][...] = colform(in_row * inv * (1.0 / D))

    def finish_da(get_c, mask_all):
        def step(rows, j, inner_rows, acc):
            inv = widen(r["colq"][rows, :])
            n = av[rows, :] * inv
            c = get_c(rows, j, inner_rows)
            da = (c * gain_row - n * widen(r["coli"][rows, :])) * inv
            g = c * n
            if mask_all:
                live = exit_of[j] > 1
                da = jnp.where(live, da, 0.0)
                g = jnp.where(live, g, 0.0)
            r["da"][rows, :] = da
            r["db"][rows, :] = da.astype(BF16)
            return acc + jnp.sum(g.reshape(RB // 8, 8, H), axis=0)

        acc = row_loop(step, jnp.zeros((8, H), F32))
        r["gz"][z] = jnp.sum(acc, axis=0, keepdims=True)
        for c in gz:
            c.start()

    def gathered_sum(name, sends, count, at, first, devices):
        buf = r[name]
        for t in range(1, count):
            src = (at + count - t) % count
            rcopy(buf.at[src], buf.at[src], r["gs"].at[first + t - 1], r["gr"].at[first + t - 1], devices[t - 1]).wait_recv()
        for c in sends:
            c.wait_send()
        total = buf[0]
        for t in range(1, count):
            total = total + buf[t]
        return total

    def vector_sends(name, at, first, devices):
        buf = r[name].at[at]
        return [rcopy(buf, buf, r["gs"].at[first + i], r["gr"].at[first + i], p) for i, p in enumerate(devices)]

    gz = vector_sends("gz", z, 0, zdev)
    gy = vector_sends("gy", y, 3, ydev)
    gx = vector_sends("gx", xl, 6, [xdev])
    gc = vector_sends("gc", s, 7, [core])

    @pl.when(s == 1)
    def _():
        cp_stat.wait_recv()
        tot = r["srow"][...] + r["rrow"][...]
        norm_columns(tot[0:1], tot[1:2])
        finish_da(lambda rows, j, ir: by_slot("cotv", j, ir, slice(None)), True)
        for c in db_out[1]:
            c.start()
        db_own(True)
        away = pl.multiple_of((1 - h) * H, 128)
        for i, (c0, cw) in enumerate(WIDE):
            r["pc"][:, c0 : c0 + cw] = lax.dot_general(
                r["db"][...], r["wv"][pl.ds(away + c0, cw), :], (((1,), (1,)), ((), ())), preferred_element_type=F32
            ).astype(BF16)
            cp_pc[i].start()
        home = pl.multiple_of(h * H, 128)
        for c0, cw in WIDE:
            r["po"][:, c0 : c0 + cw] = lax.dot_general(
                r["db"][...], r["wv"][pl.ds(home + c0, cw), :], (((1,), (1,)), ((), ())), preferred_element_type=F32
            )
        cp_po.start()
        cp_po.wait_send()
        for c in cp_pc:
            c.wait_send()

    @pl.when(s == 0)
    def _():
        cp_stat.wait_recv()
        cp_po.wait_recv()
        for c in cp_pc:
            c.wait_recv()

        def inner_step(rows, j, ir, carry):
            start = jnp.where(exit_of[j] == 1, by_slot("cotv", j, ir, slice(None)), 0.0)
            c = r["pox"][rows, :] + r["pcx"][rows, :].astype(F32) + start
            r["pox"][rows, :] = c
            r["coli"][rows, :] = lanes_sum(c * gain_row * av[rows, :])
            return carry

        row_loop(inner_step, 0)
        r["irow"][0:1, :] = rowform(r["coli"])
        cp_in.start()
        cp_in.wait()
        sq = r["srow"][0:1] + r["rrow"][0:1]
        norm_columns(sq, r["irow"][0:1] + r["irx"][0:1])
        finish_da(lambda rows, j, ir: r["pox"][rows, :], False)
        for c in db_out[0]:
            c.start()
        db_own(True)

    cp_stat.wait_send()

    own_copies(st_here, st_into, loc.at[0], r["gts"].at[0], r["gtr"].at[s, 0], False)
    relay(1, 0)
    relay(1, 1)
    wait_states(1, (0, 1, 3))
    wait_db_core(1)
    db_own(False)
    for c0, cw in PARTS:
        r["p1"][..., c0 : c0 + cw] = product(0, 3 * N, c0, cw)
    r["gy"][y] = gathered_sum("gz", gz, 4, z, 0, zdev)
    for c in gy:
        c.start()

    wait_states(0, (0, 1, 3))
    wait_db_core(0)
    relay(0, 0)
    relay(0, 1)
    for n, (c0, cw) in enumerate(PARTS):
        r["p1"][..., c0 : c0 + cw] = r["p1"][..., c0 : c0 + cw] + product(3 * N, 3 * N, c0, cw)

    wait_states(1, (2,))
    wait_states(0, (2,))
    c0, cw = PARTS[0]
    wait_far(1, 0)
    wait_far(0, 0)
    v = product(6 * N, 2 * N, c0, cw) + r["p1"][..., c0 : c0 + cw]
    r["p1"][..., c0 : c0 + cw] = v
    for q in range(4):
        r["pw0"][q] = v[:, q].astype(BF16)
    wide = []
    for t in (1, 2, 3):
        wide.append(
            rcopy(r["pw0"].at[(w + t) % 4], r["rw0"].at[t - 1], r["ws"].at[t - 1], r["wr"].at[t - 1], wdev[t - 1])
        )
        wide[-1].start()
    c0, cw = PARTS[1]
    wait_far(1, 1)
    wait_far(0, 1)
    v = product(6 * N, 2 * N, c0, cw) + r["p1"][..., c0 : c0 + cw]
    for q in range(2):
        r["ox"][q] = v[:, :, 44 * q : 44 * q + 44]
        r["px"][q] = v[:, :, 44 * q : 44 * q + 44].astype(BF16)
    cp_x = rcopy(r["px"].at[1 - xl], r["rx"], r["x3s"].at[3], r["x3r"].at[3], xdev)
    cp_x.start()
    cp_da.start()
    cp_da.wait_recv()

    def inj_step(q, carry):
        tot = []
        for j in range(2):
            rows = pl.ds(pl.multiple_of(j * R + q * RB, RB), RB)
            tot.append(r["da"][rows, :] + r["dax"][rows, :])
        rows = pl.ds(pl.multiple_of(q * RB, RB), RB)
        r["dinjv"][0, rows, :] = jnp.where(swapped, tot[1], tot[0])
        r["dinjv"][1, rows, :] = jnp.where(swapped, tot[0], tot[1])
        return carry

    lax.fori_loop(0, R // RB, inj_step, 0)
    out_inj = pltpu.make_async_copy(r["dinjv"], r["dinj"], loc.at[1])
    out_inj.start()

    cp_x.wait()
    v = r["ox"][xl] + r["rx"][...].astype(F32)
    r["ow"][...] = v
    for q in range(4):
        r["pw1"][q] = v[:, q].astype(BF16)
    narrow = []
    for t in (1, 2, 3):
        narrow.append(
            rcopy(r["pw1"].at[(w + t) % 4], r["rw1"].at[t - 1], r["ws"].at[2 + t], r["wr"].at[2 + t], wdev[t - 1])
        )
        narrow[-1].start()

    for c in st_out + db_out[0] + [cp_da]:
        c.wait_send()

    def relays_sent(n):
        for k in range(2):
            for i in range(2):
                relays[k, n, i].wait_send()

    each_piece(0, relays_sent)
    each_piece(1, relays_sent)
    r["gx"][xl] = gathered_sum("gy", gy, 4, y, 3, ydev)
    gx[0].start()

    for c in wide:
        c.wait()
    c0, cw = PARTS[0]
    v = r["p1"][:, w, :, c0 : c0 + cw]
    for t in range(3):
        v = v + r["rw0"][t].astype(F32)
    oo0, pp0, rr0 = r["oo0"], r["pp0"], r["rr0"]
    oo0[:, 0] = v[:, 0:44]
    oo0[:, 1] = v[:, 44:88]
    pp0[0] = oo0[s, 1 - xl].astype(BF16)
    pp0[1] = oo0[1 - s, 1 - xl].astype(BF16)
    last = [
        rcopy(pp0.at[0], rr0.at[0], r["x3s"].at[0], r["x3r"].at[0], xdev),
        rcopy(pp0.at[1], rr0.at[1], r["x3s"].at[1], r["x3r"].at[1], xcross),
        rcopy(oo0.at[1 - s, xl], r["rc0"], r["x3s"].at[2], r["x3r"].at[2], core),
    ]
    for c in last:
        c.start()
    r["gc"][s] = gathered_sum("gx", gx, 2, xl, 6, [xdev])
    gc[0].start()

    for c in narrow:
        c.wait()
    v = r["ow"][:, w]
    for t in range(3):
        v = v + r["rw1"][t].astype(F32)
    r["oo1"][...] = v
    cp_rc = rcopy(r["oo1"].at[1 - s], r["rc1"], r["x3s"].at[4], r["x3r"].at[4], core)
    cp_rc.start()

    stores = []

    def put(n, own, other):
        c0, cw = PARTS[n]
        low = jnp.where(s == 0, own, other)
        high = jnp.where(s == 0, other, own)
        kept = min(cw, CB - c0)
        for v, first in ((low[:, :kept], c0), (high, CB + c0)):
            cols = pl.ds(first, v.shape[1])
            r["dwv"][:, cols] = v
            stores.append(pltpu.make_async_copy(r["dwv"].at[:, cols], r["dw"].at[:, cols], loc.at[3 + len(stores)]))
            stores[-1].start()

    for c in last:
        c.wait()
    put(0, oo0[s, xl] + rr0[0].astype(F32), r["rc0"][...] + rr0[1].astype(F32))
    cp_rc.wait()
    put(1, r["oo1"][s], r["rc1"][...])
    r["dgv"][...] = gathered_sum("gc", gc, 2, s, 7, [core]).reshape(H)
    stores.append(pltpu.make_async_copy(r["dgv"], r["dg"], loc.at[8]))
    stores[-1].start()
    for c in stores + [out_inj]:
        c.wait()


def finish(dinj_ref, dw_ref, dg_ref, dinj_out, dw_out, dg_out, injv, dwv, dgv, sin, sout):
    pairs = [(dw_ref, dwv, dw_out), (dg_ref, dgv, dg_out)]
    for m in range(2):
        for q in range(0, R, 32):
            rows = (m, pl.ds(q, 32))
            pairs.append((dinj_ref.at[rows], injv.at[rows], dinj_out.at[rows]))
    loads = [pltpu.make_async_copy(a, b, sin.at[i]) for i, (a, b, _) in enumerate(pairs)]
    stores = [pltpu.make_async_copy(b, c, sout.at[i]) for i, (_, b, c) in enumerate(pairs)]
    for c in loads:
        c.start()
    for a, b in zip(loads, stores):
        a.wait()
        b.start()
    for c in stores:
        c.wait()


def shards(states, injection, cotangent, gain, weight, exits, order):
    hbm = pl.BlockSpec(memory_space=pltpu.HBM)
    vmem = pl.BlockSpec(memory_space=pltpu.VMEM)
    smem = pl.BlockSpec(memory_space=pltpu.SMEM)
    V = pltpu.VMEM
    DMA = pltpu.SemaphoreType.DMA
    ins = dict(order=smem, exits=smem, gain=hbm, states=hbm, inj=hbm, cot=hbm, w=hbm)
    outs = dict(dinj=hbm, dw=hbm, dg=hbm)
    scratch = dict(
        dinjv=V((2, R, H), F32), st=V((N, D), BF16), injv=V((2, R, H), BF16), cotv=V((2, R, H), BF16), wv=V((D, H), BF16),
        av=V((N, H), F32), colq=V((N, 128), F32), coli=V((N, 128), F32),
        srow=V((8, N), F32), rrow=V((8, N), F32), irow=V((8, N), F32), irx=V((8, N), F32),
        da=V((N, H), F32), dax=V((N, H), F32), db=V((N, H), BF16),
        po=V((N, H), F32), pox=V((N, H), F32), pc=V((N, H), BF16), pcx=V((N, H), BF16),
        stt=V((H, N), F32), stq=V((2, 4, 4, 88, N), BF16), stg=V((2, 4, 88, 8 * N), BF16),
        dbg=V((8 * N, CW), BF16), p1=V((2, 4, 88, CW), F32),
        gc=V((2, 1, H), F32), gz=V((4, 1, H), F32), gy=V((4, 1, H), F32), gx=V((2, 1, H), F32),
        d0s=DMA((3, 4)), d0r=DMA((2, 3, 4)), rls=DMA((2, 3, 2)),
        loc=DMA((12,)), gts=DMA((7,)), gtr=DMA((2, 4)), dbs=DMA, dbr=DMA((2,)),
        sts=DMA((2,)), str=DMA((2,)), das=DMA, dar=DMA, pos=DMA, por=DMA, pcs=DMA((3,)), pcr=DMA((3,)),
        ws=DMA((6,)), wr=DMA((6,)), x3s=DMA((6,)), x3r=DMA((6,)), gs=DMA((8,)), gr=DMA((8,)),
    )
    wide, narrow = PARTS[0][1], PARTS[1][1]
    scratch.update(
        pw0=V((4, 2, 88, wide), BF16), rw0=V((3, 2, 88, wide), BF16), oo0=V((2, 2, 44, wide), F32),
        pp0=V((2, 44, wide), BF16), rr0=V((2, 44, wide), BF16), rc0=V((44, wide), F32),
        ox=V((2, 2, 4, 44, narrow), F32), px=V((2, 2, 4, 44, narrow), BF16), rx=V((2, 4, 44, narrow), BF16),
        ow=V((2, 4, 44, narrow), F32), pw1=V((4, 2, 44, narrow), BF16), rw1=V((3, 2, 44, narrow), BF16),
        oo1=V((2, 44, narrow), F32), rc1=V((44, narrow), F32), dwv=V((44, H), F32), dgv=V((H,), F32), gainv=V((H,), F32),
    )
    names = list(ins) + list(outs) + list(scratch)
    dinj, dw, dg = pl.pallas_call(
        functools.partial(kernel, names),
        out_shape=(
            jax.ShapeDtypeStruct((2, R, H), F32),
            jax.ShapeDtypeStruct((44, H), F32),
            jax.ShapeDtypeStruct((H,), F32),
        ),
        in_specs=list(ins.values()),
        out_specs=tuple(outs.values()),
        scratch_shapes=list(scratch.values()),
        compiler_params=pltpu.CompilerParams(collective_id=0, has_side_effects=True, vmem_limit_bytes=65_200_000),
    )(order, exits, gain, states, injection, cotangent, weight)
    return pl.pallas_call(
        finish,
        out_shape=tuple(jax.ShapeDtypeStruct(v.shape, F32) for v in (dinj, dw, dg)),
        in_specs=[hbm] * 3,
        out_specs=(hbm,) * 3,
        scratch_shapes=[V((2, R, H), F32), V((44, H), F32), V((H,), F32), DMA((10,)), DMA((10,))],
    )(dinj, dw, dg)


def solution(mesh):
    return jax.shard_map(
        shards,
        mesh=mesh,
        in_specs=(
            P("section", "dp", None, None),
            P("dp", None, "mp"),
            P("dp", None, "mp"),
            P("mp"),
            P(None, "mp"),
            P("dp"),
            P("dp", None),
        ),
        out_specs=(P("dp", None, "mp"), P(("section", "dp"), "mp"), P("mp")),
        check_vma=False,
    )
```
